512 devices in a mesh: ind: 32 (over x, y), gene: 16 (over z, core).
Axes of the slice: x: 4, y: 8, z: 8, core: 2. Of those that a mesh axis runs over, the one named last changes fastest.
Arguments:
- genotypes: int32 [32768, 8192], P('ind', 'gene'), may hold values from 0 to 2
- covariates: float32 [20, 32768], P(None, 'ind'), may hold values from -6 to 6
- proteins: bfloat16 [32768, 1664], P('ind', 'gene'), may hold values from -6 to 6
- gene_device: int32 [32], replicated, may hold values from 0 to 15, as said below
- tile_len: int32 [32], replicated, may hold values from 16 to 128, as said below
Outputs:
- burden_z: float32 [32, 1664], P('gene', 'ind')
- skat_q: float32 [32, 1664], P('gene', 'ind')
- cov_blocks: float32 [32, 128, 128], P('gene', 'ind')
The draws below stay inside these ranges and needn't reach their ends.
Inputs may be any that keep to these rules, and one draw needn't show every extreme that they name: `gene_device`: each index of gene is named by at most 4 genes, and some are named by exactly 4. `tile_len`: some gene has all 128 variants live.
All inputs are finite; a program needn't handle non-finite values.
Results may differ from the reference program's by a relative error of at most 0.0031.
Values may be sent and summed in bfloat16 or wider, within the bound.
A program may use at most 64 MiB of HBM per device.

```python
import jax
import jax.numpy as jnp
from jax import lax

COV = 20
P_SIZE = 1664
TV = 128
GENE_DEV = 2
NIND = 32768
GENES = 32
TCAP = 4
N_GENE = 16


def ancestry_level(key):
    return jax.random.randint(jax.random.fold_in(key, 3), (NIND,), 0, 65536).astype(jnp.int32)


def covariate_rows(key):
    plasma_abundance = ancestry_level(key).astype(jnp.float32)
    key_noise, key_rest = jax.random.split(jax.random.fold_in(key, 5), 2)
    component = (plasma_abundance / 65536.0 - 0.5) * 3.1 + 0.3 * jnp.clip(jax.random.normal(key_noise, (NIND,)), -3.0, 3.0)
    rest = jnp.clip(jax.random.normal(key_rest, (COV - 1, NIND)), -6.0, 6.0)
    return jnp.concatenate([component[None, :], rest], axis=0).astype(jnp.float32)


def draw_covariates(key, part):
    return covariate_rows(key)


def draw_proteins(key, part):
    rows = covariate_rows(key)
    key_effect, key_noise = jax.random.split(jax.random.fold_in(key, 13))
    effects = 0.3 * jax.random.normal(key_effect, (COV, P_SIZE))
    effects = effects.at[0].multiply(2.0)
    levels = jax.random.normal(key_noise, (NIND, P_SIZE))
    for index in range(COV):
        levels = levels + rows[index][:, None] * effects[index][None, :]
    return jnp.clip(levels, -6.0, 6.0).astype(jnp.bfloat16)


def draw_genotypes(key, part):
    field_labels = N_GENE * TCAP * TV
    groups = field_labels // 16
    causal_share, key_shared, key_bits, key_back = jax.random.split(key, 4)
    plasma_abundance = ancestry_level(key)
    holder_share_rate = jax.random.randint(causal_share, (field_labels,), 600, 4000)
    sample_share = holder_share_rate[None, :] * (plasma_abundance[:, None] + 16384) // 49152
    shared_rate = jnp.repeat(jax.random.randint(key_shared, (groups,), 0, 1500), 16)
    random_bits = jax.random.randint(key_bits, (NIND, field_labels), 0, 2147483647)
    first_draw = random_bits % 65536
    second_draw = random_bits // 65536 * 2
    background = jnp.repeat(jax.random.randint(key_back, (NIND, groups, 2), 0, 65536), 16, axis=1)
    first_hap = ((first_draw < sample_share) | (background[:, :, 0] < shared_rate[None, :])).astype(jnp.int32)
    second_hap = ((second_draw < sample_share) | (background[:, :, 1] < shared_rate[None, :])).astype(jnp.int32)
    return first_hap + second_hap


def draw_gene_device(key, part):
    key_devices, key_genes = jax.random.split(jax.random.fold_in(key, 7))
    quarter = N_GENE // 4
    positions = jnp.arange(N_GENE, dtype=jnp.int32)
    device_loads = jnp.where(positions < quarter, 2 * GENE_DEV, jnp.where(positions < 2 * quarter, GENE_DEV, GENE_DEV // 2)).astype(jnp.int32)
    device_order = jax.random.permutation(key_devices, N_GENE).astype(jnp.int32)
    load_ends = jnp.cumsum(device_loads)
    spots = jnp.arange(GENES, dtype=jnp.int32)
    load_index = jnp.sum((spots[:, None] >= load_ends[None, :]).astype(jnp.int32), axis=1)
    owner_spot = device_order[load_index]
    gene_order = jax.random.permutation(key_genes, GENES)
    assignment = jnp.zeros((GENES,), jnp.int32).at[gene_order].set(owner_spot)
    return assignment


def draw_tile_len(key, part):
    key_len, key_full = jax.random.split(jax.random.fold_in(key, 11))
    lengths = jax.random.randint(key_len, (GENES,), 16, TV + 1)
    entire_locus = jax.random.randint(key_full, (), 0, GENES)
    return jnp.where(jnp.arange(GENES) == entire_locus, TV, lengths).astype(jnp.int32)


def setup_inputs(seed: int = 0) -> dict:
    arg_keys = jax.random.split(jax.random.key(seed), 6)
    return {
        "genotypes": draw_genotypes(jax.random.fold_in(arg_keys[5], 71), 0),
        "covariates": draw_covariates(jax.random.fold_in(arg_keys[5], 71), 0),
        "proteins": draw_proteins(jax.random.fold_in(arg_keys[5], 71), 0),
        "gene_device": draw_gene_device(jax.random.fold_in(arg_keys[5], 71), 0),
        "tile_len": draw_tile_len(jax.random.fold_in(arg_keys[5], 71), 0),
    }


highest_value = lax.Precision.HIGHEST

def solve_moments(gram_matrix, rhs):
    factor = jnp.linalg.cholesky(gram_matrix)
    return jax.scipy.linalg.cho_solve((factor, True), rhs)

def reference(genotypes, covariates, proteins, gene_device, tile_len):
    local_rows = genotypes.shape[0]
    design_width = COV + 1
    gene_order = jnp.arange(GENES, dtype=jnp.int32)
    before = (gene_device[None, :] == gene_device[:, None]) & (gene_order[None, :] < gene_order[:, None])
    slot_rank = lax.optimization_barrier(jnp.sum(before.astype(jnp.int32), axis=1)).astype(jnp.int32)
    slot_index = (gene_device * TCAP + slot_rank).astype(jnp.int32)
    geno_tiles = jnp.take(genotypes.reshape(local_rows, -1, TV), slot_index, axis=1)
    live_mask = (jnp.arange(TV, dtype=jnp.int32)[None, :] < tile_len[:, None]).astype(jnp.int32)
    allele_tally = (geno_tiles * live_mask[None]).reshape(local_rows, GENES * TV).astype(jnp.float32)
    design = jnp.concatenate([jnp.ones((1, local_rows), jnp.float32), covariates], axis=0)
    gram_matrix = jnp.dot(design, design.T, precision=highest_value)
    cross_traits = jnp.dot(design, proteins.astype(jnp.float32), precision=highest_value)
    cross_geno = jnp.dot(design, allele_tally, precision=highest_value)
    trait_coef = solve_moments(gram_matrix, cross_traits)
    geno_coef = solve_moments(gram_matrix, cross_geno)
    trait_resid = (proteins.astype(jnp.float32) - jnp.dot(design.T, trait_coef, precision=highest_value)).astype(jnp.bfloat16)
    geno_resid = (allele_tally - jnp.dot(design.T, geno_coef, precision=highest_value)).astype(jnp.bfloat16)
    allele_freq = cross_geno[0] / (2.0 * NIND)
    weight = 25.0 * (1.0 - allele_freq) ** 24 * live_mask.reshape(-1).astype(jnp.float32)
    weight_grid = weight.reshape(GENES, TV)
    scores = jnp.dot(geno_resid.T.astype(jnp.float32), trait_resid.astype(jnp.float32), preferred_element_type=jnp.float32).reshape(GENES, TV, P_SIZE)
    blocks = geno_resid.astype(jnp.float32).reshape(local_rows, GENES, TV)
    covariance = jnp.einsum('igu,igv->guv', blocks, blocks, precision=highest_value)
    square_sum = lax.optimization_barrier(jnp.sum(jnp.square(trait_resid.astype(jnp.float32)), axis=0))
    variance = square_sum / (NIND - design_width) + 1e-05
    burden_rows = jnp.einsum('igv,gv->ig', blocks, weight_grid, precision=highest_value)
    burden_den = 1.0 + lax.optimization_barrier(jnp.sum(jnp.square(burden_rows), axis=0))
    dosage_squares = lax.optimization_barrier(jnp.sum(jnp.square(blocks), axis=0))
    skat_den = 1.0 + lax.optimization_barrier(jnp.sum(weight_grid * weight_grid * dosage_squares, axis=1))
    burden_score = jnp.einsum('gvp,gv->gp', scores, weight_grid, precision=highest_value)
    skat_score = jnp.einsum('gvp,gv->gp', scores * scores, weight_grid * weight_grid, precision=highest_value)
    burden_z = burden_score / jnp.sqrt(burden_den[:, None] * variance[None, :])
    skat_q = skat_score / (skat_den[:, None] * variance[None, :])
    return (burden_z, skat_q, covariance / NIND)
```

```python
import functools

import jax
import jax.numpy as jnp
from jax import lax
from jax.experimental import pallas as pl
from jax.experimental.pallas import tpu as pltpu
from jax.sharding import PartitionSpec as P

COV = 20
WIDTH = COV + 1
TV = 128
SLOTS = 4
NX = 4
ROWS = 56
BLOCK = 64
COV_ROWS = 4
TILES = 18

BF = jnp.bfloat16
F32 = jnp.float32
HIGHEST = lax.Precision.HIGHEST
MESH = pl.DeviceIdType.MESH


def dot(a, b, form="nn", precision=None):
    dims = {"nn": ((1,), (0,)), "nt": ((1,), (1,)), "tn": ((0,), (0,))}[form]
    return lax.dot_general(a, b, (dims, ((), ())), precision=precision, preferred_element_type=F32)


def split3(v):
    hi = v.astype(BF).astype(F32)
    rest = v - hi
    mid = rest.astype(BF).astype(F32)
    return hi, mid, (rest - mid).astype(BF).astype(F32)


def iota(shape, dim):
    return lax.broadcasted_iota(jnp.int32, shape, dim)


def kernel(
    ni, ng, half, units,
    geno_ref, cov_ref, prot_ref, mask_ref, pick_ref,
    bz_ref, sq_ref, cv_ref,
    g_s, gb_s, gr_s, d_s, dst_s, dct_s, tall, stat_s, part_s, psum_s, total_s, call_s,
    ext_s, p_s, sbuf, relay_in, relay_out, from_one, from_two, yout, yin, fin_s, fall,
    load_sem, t_send, t_recv, pair_send, pair_recv, own_send, own_recv,
    rs_send, rs_recv, ag_send, ag_recv, c_send, c_recv, x_send, x_recv, y_send, y_recv,
    f_send, f_recv,
):
    ind, gene = lax.axis_index("ind"), lax.axis_index("gene")
    ny, nz = ni // NX, ng // 2
    x, y = lax.div(ind, ny), lax.rem(ind, ny)
    z, core = lax.div(gene, 2), lax.rem(gene, 2)
    rows, pt = prot_ref.shape
    half_rows = rows // 2
    per_chunk = ni // ng
    n_total = rows * ni
    lanes = SLOTS * TV
    per_unit = TILES // units

    def remote(src, dst, send, recv, i, g):
        return pltpu.make_async_remote_copy(
            src_ref=src, dst_ref=dst, send_sem=send, recv_sem=recv,
            device_id=(i, g), device_id_type=MESH,
        )

    load = pltpu.make_async_copy(geno_ref, g_s, load_sem)
    load.start()
    barrier = pltpu.get_barrier_semaphore()

    @pl.loop(1, ni)
    def _(d):
        pl.semaphore_signal(
            barrier, inc=1, device_id=(lax.rem(ind + d, ni), gene), device_id_type=MESH
        )

    @pl.loop(1, ng)
    def _(d):
        pl.semaphore_signal(
            barrier, inc=1, device_id=(ind, lax.rem(gene + d, ng)), device_id_type=MESH
        )

    eye = (iota((pt, pt), 0) == iota((pt, pt), 1)).astype(F32).astype(BF)
    tt = dot(eye, prot_ref[...], "nt").astype(BF)
    tall[gene, 0] = tt[:, :half_rows]
    tall[gene, 1] = tt[:, half_rows:]
    pl.semaphore_wait(barrier, ni + ng - 2)

    def ring(way, step, q):
        sign = 1 if way == 0 else -1
        chunk = lax.rem(z - sign * (step - 1) + 2 * nz, nz) * 2 + core
        target = lax.rem(z + sign + nz, nz) * 2 + core
        return remote(
            tall.at[chunk, q], tall.at[chunk, q],
            t_send.at[way, step - 1, q], t_recv.at[way, step - 1, q], ind, target,
        )

    def across(way, step, q):
        sign = 1 if way == 0 else -1
        chunk = lax.rem(z - sign * step + 2 * nz, nz) * 2 + core
        return remote(
            tall.at[chunk, q], tall.at[chunk, q],
            pair_send.at[way, step - 1, q], pair_recv.at[way, step - 1, q],
            ind, z * 2 + 1 - core,
        )

    def moves(step):
        if step < nz // 2:
            return [(way, q) for q in range(2) for way in range(2)]
        return [(0, 0), (1, 1)]

    own_copy = remote(tall.at[gene], tall.at[gene], own_send, own_recv, ind, z * 2 + 1 - core)
    for way, q in moves(1):
        ring(way, 1, q).start()
    own_copy.start()

    def forward(step):
        for way, q in moves(step):
            ring(way, step, q).wait_recv()
            if step < nz // 2 and (way, q) in moves(step + 1):
                ring(way, step + 1, q).start()
            across(way, step, q).start()

    d_s[...] = jnp.zeros_like(d_s)
    d_s[0:1, :] = jnp.ones((1, rows), F32)
    d_s[1 : 1 + COV, :] = cov_ref[...]
    design = d_s[...]
    d1, d2, d3 = split3(design)
    dst_s[...] = jnp.concatenate([d1, d2, d3], axis=0).astype(BF)
    mask = mask_ref[...]
    load.wait()
    step_rows = min(128, rows)

    @pl.loop(0, rows // step_rows)
    def _(b):
        at = pl.ds(pl.multiple_of(b * step_rows, step_rows), step_rows)
        gb_s[at, :] = (g_s[at, :].astype(F32) * mask).astype(BF)

    wide = dot(dst_s[...], gb_s[...])
    dg = wide[0:32] + wide[32:64] + wide[64:96]
    tall_own = jnp.concatenate([tall[gene, 0], tall[gene, 1]], axis=1)
    narrow = dot(dst_s[...], tall_own, "nt")
    dt = narrow[0:32] + narrow[32:64] + narrow[64:96]
    square = jnp.square(tall_own.astype(F32))
    sq_hi = square.astype(BF)
    sq_lo = (square - sq_hi.astype(F32)).astype(BF)
    ones = jnp.ones((16, rows), BF)
    t2 = dot(ones, sq_hi, "nt") + dot(ones, sq_lo, "nt")
    dt = dt[0:24] + jnp.where(iota((24, pt), 0) == WIDTH, t2[0:1], 0.0)
    gram = dot(design, design, "nt", HIGHEST)
    stat_s[...] = jnp.zeros_like(stat_s)
    for r in range(3):
        sub = slice(8 * r, 8 * r + 8)
        for c in range(SLOTS):
            k = r * SLOTS + c
            at = slice(8 * (k % per_unit), 8 * (k % per_unit) + 8)
            stat_s[k // per_unit, at, :] = dg[sub, TV * c : TV * c + TV]
        k = 12 + r
        at = slice(8 * (k % per_unit), 8 * (k % per_unit) + 8)
        stat_s[k // per_unit, at, 0:pt] = dt[sub]
        k = 15 + r
        at = slice(8 * (k % per_unit), 8 * (k % per_unit) + 8)
        stat_s[k // per_unit, at, 0:32] = gram[sub]

    def to_owner(t):
        return remote(
            stat_s.at[t], part_s.at[lax.rem(ind - t + ni, ni)], rs_send, rs_recv, t, gene
        )

    @pl.loop(0, units)
    def _(t):
        @pl.when(t != ind)
        def _():
            to_owner(t).start()

    dcat = jnp.concatenate([d1, d2, d3, d1, d2, d1, jnp.zeros((64, rows), F32)], axis=0)
    dct_s[...] = jnp.transpose(dcat).astype(BF)
    forward(1)

    @pl.when(ind < units)
    def _():
        part_s[0] = stat_s[ind]
        got = part_s.at[pl.ds(1, ni - 1)]
        remote(got, got, rs_send, rs_recv, ind, gene).wait_recv()
        subtotal = jnp.sum(part_s[...], axis=0)
        psum_s[...] = subtotal
        total_s[ind] = subtotal

        @pl.loop(1, ni)
        def _(d):
            remote(
                psum_s, total_s.at[ind], ag_send, ag_recv, lax.rem(ind + d, ni), gene
            ).start()

    if nz // 2 >= 2:
        forward(2)

    @pl.when(ind < units)
    def _():
        got = total_s.at[pl.ds(0, units - 1)]
        remote(got, got, ag_send, ag_recv, ind, gene).wait_recv()

    @pl.when(ind >= units)
    def _():
        remote(total_s, total_s, ag_send, ag_recv, ind, gene).wait_recv()

    def tile(k):
        return total_s[k // per_unit, 8 * (k % per_unit) : 8 * (k % per_unit) + 8, :]

    cross_geno = jnp.concatenate(
        [jnp.concatenate([tile(r * SLOTS + c) for c in range(SLOTS)], axis=1) for r in range(3)],
        axis=0,
    )
    traits = jnp.concatenate([tile(12 + r) for r in range(3)], axis=0)
    gram_sum = jnp.concatenate([tile(15 + r) for r in range(3)], axis=0)
    t2_sum = traits[WIDTH : WIDTH + 1]
    cross_traits = jnp.where(iota((24, TV), 0) < WIDTH, traits, 0.0)
    work = jnp.concatenate([gram_sum, cross_geno, cross_traits], axis=1)
    row_id = iota(work.shape, 0)
    for k in range(WIDTH):
        pivot = work[k : k + 1] / work[k : k + 1, k : k + 1]
        work = jnp.where(row_id == k, pivot, work - work[:, k : k + 1] * pivot)
    geno_coef = work[:, TV : TV + lanes]
    trait_coef = work[:, TV + lanes :]
    variance = (t2_sum - jnp.sum(cross_traits * trait_coef, axis=0, keepdims=True)) / (
        n_total - WIDTH
    ) + 1e-05
    v1, v2, v3 = split3(variance)
    sub8 = iota((8, TV), 0)
    tail = jnp.where(sub8 == 0, v1, jnp.where(sub8 == 1, v2, jnp.where(sub8 == 2, v3, 0.0)))
    call_s[gene] = jnp.concatenate([trait_coef, tail], axis=0).astype(BF)

    @pl.loop(1, ng)
    def _(d):
        remote(
            call_s.at[gene], call_s.at[gene], c_send, c_recv, ind, lax.rem(gene + d, ng)
        ).start()

    if nz // 2 >= 3:
        forward(3)
    base = 1.0 - cross_geno[0:1] / (2.0 * n_total)
    b2 = base * base
    b4 = b2 * b2
    b8 = b4 * b4
    weight = 25.0 * (b8 * b8 * b8) * mask

    c1, c2, c3 = split3(jnp.concatenate([geno_coef, jnp.zeros((8, lanes), F32)], axis=0))
    rcat = jnp.concatenate([c1, c1, c1, c2, c2, c3, jnp.zeros((64, lanes), F32)], axis=0).astype(BF)

    @pl.loop(0, rows // step_rows)
    def _(b):
        at = pl.ds(pl.multiple_of(b * step_rows, step_rows), step_rows)
        gr_s[at, :] = (gb_s[at, :].astype(F32) - dot(dct_s[at, :], rcat)).astype(BF)

    wide = dot(dst_s[...], gr_s[...])
    h1, h2, h3 = split3(wide[0:32] + wide[32:64] + wide[64:96])
    hcat = jnp.concatenate([h1, h2, h3], axis=0).astype(BF)

    sel_r, sel_c = iota((ni * 8, TV), 0), iota((ni * 8, TV), 1)
    sub = lax.rem(sel_r, 8)
    sel = jnp.where((sub < COV_ROWS) & (sel_c == lax.div(sel_r, 8) * COV_ROWS + sub), 1.0, 0.0)
    sel = sel.astype(BF)
    diag = iota((TV, TV), 0) == iota((TV, TV), 1)
    for s in range(SLOTS):
        cols = slice(s * TV, s * TV + TV)
        tile_r = gr_s[:, cols]
        cov_s = dot(tile_r, tile_r, "tn")
        w = weight[:, cols]
        wc = dot(jnp.broadcast_to(w, (8, TV)), cov_s, "nn", HIGHEST)
        burden = jnp.sum(wc[0:1] * w, axis=1, keepdims=True)
        dosage = jnp.sum(jnp.where(diag, cov_s, 0.0), axis=0, keepdims=True)
        skat = jnp.sum(dosage * w * w, axis=1, keepdims=True)
        b_hi, b_lo, _ = split3(burden)
        k_hi, k_lo, _ = split3(skat)
        ext = dot(sel, cov_s.astype(BF))
        ext = jnp.where(sub == 4, b_hi, jnp.where(sub == 5, b_lo, ext))
        ext = jnp.where(sub == 6, k_hi, jnp.where(sub == 7, k_lo, ext))
        ext_s[s] = ext.reshape(ni, 8, TV)

    for step in range(4, nz // 2 + 1):
        forward(step)
    got = call_s.at[pl.ds(0, ng - 1)]
    remote(got, got, c_send, c_recv, ind, gene).wait_recv()
    own_copy.wait_recv()
    for step in range(1, nz // 2 + 1):
        for way, q in moves(step):
            across(way, step, q).wait_recv()

    p_s[...] = jnp.zeros_like(p_s)

    @pl.loop(0, ng)
    def _(j):
        cj = call_s[j]
        fix = dot(jnp.concatenate([cj, cj, cj], axis=0), hcat, "tn")
        p_s[0:pt, :] = (
            dot(tall[j, 0], gr_s[0:half_rows, :])
            + dot(tall[j, 1], gr_s[half_rows:, :])
            - fix[0:pt]
        )
        for kk in range(per_chunk):
            i = j * per_chunk + kk
            for s in range(SLOTS):
                part = p_s[kk * half : kk * half + ROWS, s * TV : s * TV + TV]
                sbuf[s, i] = jnp.concatenate([part, ext_s[s, i]], axis=0).astype(BF)

    def unit(s, to):
        return sbuf.at[s, pl.ds(lax.rem(to + NX, NX) * ny, ny)]

    def x_copy(s, which):
        sign = 1 if s % 2 == 0 else -1
        ahead = lax.rem(x + sign + NX, NX) * ny + y
        behind = lax.rem(x - sign + NX, NX) * ny + y
        src, dst, to = (
            (lambda: unit(s, x + 2), relay_in, ahead),
            (lambda: unit(s, x - sign), from_one, behind),
            (lambda: relay_out.at[s], from_two, ahead),
        )[which]
        return remote(src(), dst.at[s], x_send.at[s, which], x_recv.at[s, which], to, gene)

    def y_copy(s, d):
        to = lax.rem(y + d, ny)
        return remote(
            yout.at[s, to], yin.at[s, ny - d], y_send.at[s], y_recv.at[s], x * ny + to, gene
        )

    def relay(s):
        sign = 1 if s % 2 == 0 else -1
        x_copy(s, 0).wait_recv()
        to = lax.rem(x + sign + NX, NX) * ny

        @pl.loop(0, ny)
        def _(b):
            relay_out[s, b] = (relay_in[s, b].astype(F32) + sbuf[s, to + b].astype(F32)).astype(BF)

        x_copy(s, 2).start()

    def over_x(s, b):
        return (
            sbuf[s, x * ny + b].astype(F32)
            + from_one[s, b].astype(F32)
            + from_two[s, b].astype(F32)
        )

    def gather_x(s):
        x_copy(s, 1).wait_recv()
        x_copy(s, 2).wait_recv()

        @pl.loop(0, ny)
        def _(b):
            yout[s, b] = over_x(s, b).astype(BF)

        @pl.loop(1, ny)
        def _(d):
            y_copy(s, d).start()

    for s in range(SLOTS):
        x_copy(s, 0).start()
        x_copy(s, 1).start()
    relay(0)
    relay(1)
    gather_x(0)
    relay(2)
    gather_x(1)
    relay(3)
    gather_x(2)
    gather_x(3)

    vrow = call_s[lax.div(ind, per_chunk)].astype(F32)[24:32]
    vrow = jnp.broadcast_to(vrow[0:1] + vrow[1:2] + vrow[2:3], (8, TV))
    var = vrow
    for kk in range(1, per_chunk):
        var = jnp.where(lax.rem(ind, per_chunk) == kk, pltpu.roll(vrow, TV - kk * half, 1), var)
    var = var[0:1, 0:ROWS]
    fin_s[...] = jnp.zeros_like(fin_s)
    for s in range(SLOTS):
        got = yin.at[s, pl.ds(1, ny - 1)]
        remote(got, got, y_send.at[s], y_recv.at[s], ind, gene).wait_recv()
        whole = over_x(s, y)
        for d in range(1, ny):
            whole = whole + yin[s, d].astype(F32)
        score = whole[0:ROWS]
        w = jnp.broadcast_to(weight[:, s * TV : s * TV + TV], (8, TV))
        burden = dot(w, score, "nt", HIGHEST)[0:1]
        skat = dot(w * w, score * score, "nt", HIGHEST)[0:1]
        b_den = 1.0 + whole[60:61, 0:ROWS] + whole[61:62, 0:ROWS]
        k_den = 1.0 + whole[62:63, 0:ROWS] + whole[63:64, 0:ROWS]
        fin_s[s : s + 1, 0:ROWS] = burden / jnp.sqrt(b_den * var)
        fin_s[4 + s : 5 + s, 0:ROWS] = skat / (k_den * var)
        up = 4 * (s // 2)
        left = TV + TV * (s % 2)
        fin_s[up : up + 4, left : left + TV] = whole[56:60] * (1.0 / n_total)

    @pl.loop(1, ng)
    def _(d):
        remote(fin_s, fall.at[ng - d], f_send, f_recv, ind, lax.rem(gene + d, ng)).start()

    fall[0] = fin_s[...]
    got = fall.at[pl.ds(1, ng - 1)]
    remote(got, got, f_send, f_recv, ind, gene).wait_recv()
    flat = fall[...].reshape(ng * 8, 3 * TV)
    stats = dot(pick_ref[0:8], flat[:, 0:TV], "nn", HIGHEST)
    bz_ref[...] = stats[0:2, 0:half]
    sq_ref[...] = stats[2:4, 0:half]
    cov_out = dot(pick_ref[8:16], flat[:, TV : 2 * TV], "nn", HIGHEST) + dot(
        pick_ref[16:24], flat[:, 2 * TV :], "nn", HIGHEST
    )
    cv_ref[0] = cov_out[0:4]
    cv_ref[1] = cov_out[4:8]

    for step in range(1, nz // 2 + 1):
        for way, q in moves(step):
            ring(way, step, q).wait_send()
            across(way, step, q).wait_send()
    own_copy.wait_send()

    @pl.when(ind < units)
    def _():
        got = stat_s.at[pl.ds(0, units - 1)]
        remote(got, got, rs_send, rs_recv, ind, gene).wait_send()
        got = part_s.at[pl.ds(1, ni - 1)]
        remote(got, got, ag_send, ag_recv, ind, gene).wait_send()

    @pl.when(ind >= units)
    def _():
        remote(stat_s, stat_s, rs_send, rs_recv, ind, gene).wait_send()

    got = call_s.at[pl.ds(0, ng - 1)]
    remote(got, got, c_send, c_recv, ind, gene).wait_send()
    for s in range(SLOTS):
        for which in range(3):
            x_copy(s, which).wait_send()
        got = yout.at[s, pl.ds(0, ny - 1)]
        remote(got, got, y_send.at[s], y_recv.at[s], ind, gene).wait_send()
    got = fall.at[pl.ds(1, ng - 1)]
    remote(got, got, f_send, f_recv, ind, gene).wait_send()


def selections(gene_device, tile_len, gene_axis, owned):
    me = lax.axis_index("gene")
    total = gene_device.shape[0]
    order = jnp.arange(total, dtype=jnp.int32)
    before = (gene_device[None, :] == gene_device[:, None]) & (order[None, :] < order[:, None])
    rank = jnp.sum(before.astype(jnp.int32), axis=1)
    slot = jnp.arange(SLOTS * TV, dtype=jnp.int32) // TV
    variant = jnp.arange(SLOTS * TV, dtype=jnp.int32) % TV
    live = (
        (gene_device[:, None] == me)
        & (rank[:, None] == slot[None, :])
        & (variant[None, :] < tile_len[:, None])
    )
    mask = jnp.any(live, axis=0).astype(F32)[None, :]
    mine = order[None, :] == (me * owned + jnp.arange(owned, dtype=jnp.int32))[:, None]
    where = jnp.sum(jnp.where(mine, lax.rem(gene_device - me + gene_axis, gene_axis), 0), axis=1)
    slot_of = jnp.sum(jnp.where(mine, rank, 0), axis=1)
    r = jnp.arange(24, dtype=jnp.int32)[:, None]
    gene_row = jnp.where(r < 8, r % 2, (r - 8) % 8 // 4)
    here = jnp.where(gene_row == 0, where[0], where[1])
    s = jnp.where(gene_row == 0, slot_of[0], slot_of[1])
    stat_col = here * 8 + jnp.where(r < 2, s, 4 + s)
    cov_col = here * 8 + s // 2 * 4 + (r - 8) % 4
    cov_on = s % 2 == (r - 8) // 8
    col = jnp.where(r < 8, stat_col, cov_col)
    on = jnp.where(r < 8, r < 4, cov_on)
    wide = jnp.arange(gene_axis * 8, dtype=jnp.int32)[None, :]
    pick = ((wide == col) & on).astype(F32)
    return mask, pick


def per_device(genotypes, covariates, proteins, gene_device, tile_len):
    ni, ng = lax.axis_size("ind"), lax.axis_size("gene")
    rows, pt = proteins.shape
    lanes = SLOTS * TV
    half = pt * ng // ni
    owned = gene_device.shape[0] // ng
    units = TILES if ni >= TILES else 6
    tall_unit = TILES // units * 8
    ny, nz = ni // NX, ng // 2
    mask, pick = selections(gene_device, tile_len, ng, owned)
    vmem = pl.BlockSpec(memory_space=pltpu.VMEM)
    dma = pltpu.SemaphoreType.DMA
    unit = (SLOTS, ny, BLOCK, TV)
    scratch = [
        pltpu.VMEM((rows, lanes), jnp.int32),
        pltpu.VMEM((rows, lanes), BF),
        pltpu.VMEM((rows, lanes), BF),
        pltpu.VMEM((32, rows), F32),
        pltpu.VMEM((96, rows), BF),
        pltpu.VMEM((rows, 256), BF),
        pltpu.VMEM((ng, 2, pt, rows // 2), BF),
        pltpu.VMEM((units, tall_unit, TV), F32),
        pltpu.VMEM((ni, tall_unit, TV), F32),
        pltpu.VMEM((tall_unit, TV), F32),
        pltpu.VMEM((units, tall_unit, TV), F32),
        pltpu.VMEM((ng, 32, TV), BF),
        pltpu.VMEM((SLOTS, ni, 8, TV), F32),
        pltpu.VMEM((112, lanes), F32),
        pltpu.VMEM((SLOTS, ni, BLOCK, TV), BF),
        pltpu.VMEM(unit, BF),
        pltpu.VMEM(unit, BF),
        pltpu.VMEM(unit, BF),
        pltpu.VMEM(unit, BF),
        pltpu.VMEM(unit, BF),
        pltpu.VMEM(unit, BF),
        pltpu.VMEM((8, 3 * TV), F32),
        pltpu.VMEM((ng, 8, 3 * TV), F32),
        dma,
        dma((2, nz // 2, 2)), dma((2, nz // 2, 2)),
        dma((2, nz // 2, 2)), dma((2, nz // 2, 2)),
        dma, dma, dma, dma, dma, dma, dma, dma,
        dma((SLOTS, 3)), dma((SLOTS, 3)),
        dma((SLOTS,)), dma((SLOTS,)),
        dma, dma,
    ]
    return pl.pallas_call(
        functools.partial(kernel, ni, ng, half, units),
        out_shape=(
            jax.ShapeDtypeStruct((owned, half), F32),
            jax.ShapeDtypeStruct((owned, half), F32),
            jax.ShapeDtypeStruct((owned, COV_ROWS, TV), F32),
        ),
        in_specs=[pl.BlockSpec(memory_space=pl.ANY), vmem, vmem, vmem, vmem],
        out_specs=(vmem, vmem, vmem),
        scratch_shapes=scratch,
        compiler_params=pltpu.CompilerParams(
            collective_id=0, has_side_effects=True, vmem_limit_bytes=48 * 1024 * 1024
        ),
    )(genotypes, covariates, proteins, mask, pick)


def solution(mesh):
    return jax.shard_map(
        per_device,
        mesh=mesh,
        in_specs=(P("ind", "gene"), P(None, "ind"), P("ind", "gene"), P(), P()),
        out_specs=(P("gene", "ind"), P("gene", "ind"), P("gene", "ind", None)),
        check_vma=False,
    )
```

```python
import functools

import jax
import jax.numpy as jnp
from jax import lax
from jax.experimental import pallas as pl
from jax.experimental.pallas import tpu as pltpu
from jax.sharding import PartitionSpec as P

COV = 20
WIDTH = COV + 1
TV = 128
SLOTS = 4
NX = 4
ROWS = 56
BLOCK = 64
COV_ROWS = 4
TILES = 18

BF = jnp.bfloat16
F32 = jnp.float32
HIGHEST = lax.Precision.HIGHEST
MESH = pl.DeviceIdType.MESH


def dot(a, b, form="nn", precision=None):
    dims = {"nn": ((1,), (0,)), "nt": ((1,), (1,)), "tn": ((0,), (0,))}[form]
    return lax.dot_general(a, b, (dims, ((), ())), precision=precision, preferred_element_type=F32)


def split3(v):
    hi = v.astype(BF).astype(F32)
    rest = v - hi
    mid = rest.astype(BF).astype(F32)
    return hi, mid, (rest - mid).astype(BF).astype(F32)


def iota(shape, dim):
    return lax.broadcasted_iota(jnp.int32, shape, dim)


def kernel(
    ni, ng, half, units,
    geno_ref, cov_ref, prot_ref, home_ref, len_ref,
    bz_ref, sq_ref, cv_ref,
    g_s, gb_s, gr_s, d_s, dst_s, dct_s, tall, stat_s, part_s, psum_s, total_s, call_s,
    ext_s, p_s, sbuf, relay_in, relay_out, from_one, from_two, yout, yin, fin_s, fall,
    load_sem, t_send, t_recv, pair_send, pair_recv, own_send, own_recv,
    rs_send, rs_recv, ag_send, ag_recv, c_send, c_recv, x_send, x_recv, y_send, y_recv,
    f_send, f_recv,
):
    ind, gene = lax.axis_index("ind"), lax.axis_index("gene")
    ny, nz = ni // NX, ng // 2
    x, y = lax.div(ind, ny), lax.rem(ind, ny)
    z, core = lax.div(gene, 2), lax.rem(gene, 2)
    pt, rows = prot_ref.shape
    half_rows = rows // 2
    per_chunk = ni // ng
    n_total = rows * ni
    lanes = SLOTS * TV
    per_unit = TILES // units

    def remote(src, dst, send, recv, i, g):
        return pltpu.make_async_remote_copy(
            src_ref=src, dst_ref=dst, send_sem=send, recv_sem=recv,
            device_id=(i, g), device_id_type=MESH,
        )

    load = pltpu.make_async_copy(geno_ref, g_s, load_sem)
    load.start()
    barrier = pltpu.get_barrier_semaphore()

    @pl.loop(1, ni)
    def _(d):
        pl.semaphore_signal(
            barrier, inc=1, device_id=(lax.rem(ind + d, ni), gene), device_id_type=MESH
        )

    @pl.loop(1, ng)
    def _(d):
        pl.semaphore_signal(
            barrier, inc=1, device_id=(ind, lax.rem(gene + d, ng)), device_id_type=MESH
        )

    tall[gene, 0] = prot_ref[:, :half_rows]
    tall[gene, 1] = prot_ref[:, half_rows:]
    mask, pick = selections(home_ref[...], len_ref[...], gene, ng)
    pl.semaphore_wait(barrier, ni + ng - 2)

    def ring(way, step, q):
        sign = 1 if way == 0 else -1
        chunk = lax.rem(z - sign * (step - 1) + 2 * nz, nz) * 2 + core
        target = lax.rem(z + sign + nz, nz) * 2 + core
        return remote(
            tall.at[chunk, q], tall.at[chunk, q],
            t_send.at[way, step - 1, q], t_recv.at[way, step - 1, q], ind, target,
        )

    def across(way, step, q):
        sign = 1 if way == 0 else -1
        chunk = lax.rem(z - sign * step + 2 * nz, nz) * 2 + core
        return remote(
            tall.at[chunk, q], tall.at[chunk, q],
            pair_send.at[way, step - 1, q], pair_recv.at[way, step - 1, q],
            ind, z * 2 + 1 - core,
        )

    def moves(step):
        if step < nz // 2:
            return [(way, q) for q in range(2) for way in range(2)]
        return [(0, 0), (1, 1)]

    own_copy = remote(tall.at[gene], tall.at[gene], own_send, own_recv, ind, z * 2 + 1 - core)
    for way, q in moves(1):
        ring(way, 1, q).start()
    own_copy.start()

    def forward(step):
        for way, q in moves(step):
            ring(way, step, q).wait_recv()
            if step < nz // 2 and (way, q) in moves(step + 1):
                ring(way, step + 1, q).start()
            across(way, step, q).start()

    d_s[...] = jnp.zeros_like(d_s)
    d_s[0:1, :] = jnp.ones((1, rows), F32)
    d_s[1 : 1 + COV, :] = cov_ref[...]
    design = d_s[...]
    d1, d2, d3 = split3(design)
    dst_s[...] = jnp.concatenate([d1, d2, d3], axis=0).astype(BF)
    load.wait()
    step_rows = min(128, rows)

    @pl.loop(0, rows // step_rows)
    def _(b):
        at = pl.ds(pl.multiple_of(b * step_rows, step_rows), step_rows)
        gb_s[at, :] = (g_s[at, :].astype(F32) * mask).astype(BF)

    wide = dot(dst_s[...], gb_s[...])
    dg = wide[0:32] + wide[32:64] + wide[64:96]
    tall_own = prot_ref[...]
    narrow = dot(dst_s[...], tall_own, "nt")
    dt = narrow[0:32] + narrow[32:64] + narrow[64:96]
    square = jnp.square(tall_own.astype(F32))
    sq_hi = square.astype(BF)
    sq_lo = (square - sq_hi.astype(F32)).astype(BF)
    ones = jnp.ones((16, rows), BF)
    t2 = dot(ones, sq_hi, "nt") + dot(ones, sq_lo, "nt")
    dt = dt[0:24] + jnp.where(iota((24, pt), 0) == WIDTH, t2[0:1], 0.0)
    gram = dot(design, design, "nt", HIGHEST)
    stat_s[...] = jnp.zeros_like(stat_s)
    for r in range(3):
        sub = slice(8 * r, 8 * r + 8)
        for c in range(SLOTS):
            k = r * SLOTS + c
            at = slice(8 * (k % per_unit), 8 * (k % per_unit) + 8)
            stat_s[k // per_unit, at, :] = dg[sub, TV * c : TV * c + TV]
        k = 12 + r
        at = slice(8 * (k % per_unit), 8 * (k % per_unit) + 8)
        stat_s[k // per_unit, at, 0:pt] = dt[sub]
        k = 15 + r
        at = slice(8 * (k % per_unit), 8 * (k % per_unit) + 8)
        stat_s[k // per_unit, at, 0:32] = gram[sub]

    def to_owner(t):
        return remote(
            stat_s.at[t], part_s.at[lax.rem(ind - t + ni, ni)], rs_send, rs_recv, t, gene
        )

    @pl.loop(0, units)
    def _(t):
        @pl.when(t != ind)
        def _():
            to_owner(t).start()

    dcat = jnp.concatenate([d1, d2, d3, d1, d2, d1, jnp.zeros((64, rows), F32)], axis=0)
    dct_s[...] = jnp.transpose(dcat).astype(BF)
    forward(1)

    @pl.when(ind < units)
    def _():
        part_s[0] = stat_s[ind]
        got = part_s.at[pl.ds(1, ni - 1)]
        remote(got, got, rs_send, rs_recv, ind, gene).wait_recv()
        subtotal = jnp.sum(part_s[...], axis=0)
        psum_s[...] = subtotal
        total_s[ind] = subtotal

        @pl.loop(1, ni)
        def _(d):
            remote(
                psum_s, total_s.at[ind], ag_send, ag_recv, lax.rem(ind + d, ni), gene
            ).start()

    if nz // 2 >= 2:
        forward(2)

    @pl.when(ind < units)
    def _():
        got = total_s.at[pl.ds(0, units - 1)]
        remote(got, got, ag_send, ag_recv, ind, gene).wait_recv()

    @pl.when(ind >= units)
    def _():
        remote(total_s, total_s, ag_send, ag_recv, ind, gene).wait_recv()

    def tile(k):
        return total_s[k // per_unit, 8 * (k % per_unit) : 8 * (k % per_unit) + 8, :]

    cross_geno = jnp.concatenate(
        [jnp.concatenate([tile(r * SLOTS + c) for c in range(SLOTS)], axis=1) for r in range(3)],
        axis=0,
    )
    traits = jnp.concatenate([tile(12 + r) for r in range(3)], axis=0)
    gram_sum = jnp.concatenate([tile(15 + r) for r in range(3)], axis=0)
    t2_sum = traits[WIDTH : WIDTH + 1]
    cross_traits = jnp.where(iota((24, TV), 0) < WIDTH, traits, 0.0)
    work = jnp.concatenate([gram_sum, cross_geno, cross_traits], axis=1)
    row_id = iota(work.shape, 0)
    for k in range(WIDTH):
        pivot = work[k : k + 1] / work[k : k + 1, k : k + 1]
        work = jnp.where(row_id == k, pivot, work - work[:, k : k + 1] * pivot)
    geno_coef = work[:, TV : TV + lanes]
    trait_coef = work[:, TV + lanes :]
    variance = (t2_sum - jnp.sum(cross_traits * trait_coef, axis=0, keepdims=True)) / (
        n_total - WIDTH
    ) + 1e-05
    v1, v2, v3 = split3(variance)
    sub8 = iota((8, TV), 0)
    tail = jnp.where(sub8 == 0, v1, jnp.where(sub8 == 1, v2, jnp.where(sub8 == 2, v3, 0.0)))
    call_s[gene] = jnp.concatenate([trait_coef, tail], axis=0).astype(BF)

    @pl.loop(1, ng)
    def _(d):
        remote(
            call_s.at[gene], call_s.at[gene], c_send, c_recv, ind, lax.rem(gene + d, ng)
        ).start()

    if nz // 2 >= 3:
        forward(3)
    base = 1.0 - cross_geno[0:1] / (2.0 * n_total)
    b2 = base * base
    b4 = b2 * b2
    b8 = b4 * b4
    weight = 25.0 * (b8 * b8 * b8) * mask

    c1, c2, c3 = split3(jnp.concatenate([geno_coef, jnp.zeros((8, lanes), F32)], axis=0))
    rcat = jnp.concatenate([c1, c1, c1, c2, c2, c3, jnp.zeros((64, lanes), F32)], axis=0).astype(BF)

    @pl.loop(0, rows // step_rows)
    def _(b):
        at = pl.ds(pl.multiple_of(b * step_rows, step_rows), step_rows)
        gr_s[at, :] = (gb_s[at, :].astype(F32) - dot(dct_s[at, :], rcat)).astype(BF)

    wide = dot(dst_s[...], gr_s[...])
    h1, h2, h3 = split3(wide[0:32] + wide[32:64] + wide[64:96])
    hcat = jnp.concatenate([h1, h2, h3], axis=0).astype(BF)

    sel_r, sel_c = iota((ni * 8, TV), 0), iota((ni * 8, TV), 1)
    sub = lax.rem(sel_r, 8)
    sel = jnp.where((sub < COV_ROWS) & (sel_c == lax.div(sel_r, 8) * COV_ROWS + sub), 1.0, 0.0)
    sel = sel.astype(BF)
    diag = iota((TV, TV), 0) == iota((TV, TV), 1)
    for s in range(SLOTS):
        cols = slice(s * TV, s * TV + TV)
        tile_r = gr_s[:, cols]
        cov_s = dot(tile_r, tile_r, "tn")
        w = weight[:, cols]
        wc = dot(jnp.broadcast_to(w, (8, TV)), cov_s, "nn", HIGHEST)
        burden = jnp.sum(wc[0:1] * w, axis=1, keepdims=True)
        dosage = jnp.sum(jnp.where(diag, cov_s, 0.0), axis=0, keepdims=True)
        skat = jnp.sum(dosage * w * w, axis=1, keepdims=True)
        b_hi, b_lo, _ = split3(burden)
        k_hi, k_lo, _ = split3(skat)
        ext = dot(sel, cov_s.astype(BF))
        ext = jnp.where(sub == 4, b_hi, jnp.where(sub == 5, b_lo, ext))
        ext = jnp.where(sub == 6, k_hi, jnp.where(sub == 7, k_lo, ext))
        ext_s[s] = ext.reshape(ni, 8, TV)

    for step in range(4, nz // 2 + 1):
        forward(step)
    got = call_s.at[pl.ds(0, ng - 1)]
    remote(got, got, c_send, c_recv, ind, gene).wait_recv()
    own_copy.wait_recv()
    for step in range(1, nz // 2 + 1):
        for way, q in moves(step):
            across(way, step, q).wait_recv()

    p_s[...] = jnp.zeros_like(p_s)

    @pl.loop(0, ng)
    def _(j):
        cj = call_s[j]
        fix = dot(jnp.concatenate([cj, cj, cj], axis=0), hcat, "tn")
        p_s[0:pt, :] = (
            dot(tall[j, 0], gr_s[0:half_rows, :])
            + dot(tall[j, 1], gr_s[half_rows:, :])
            - fix[0:pt]
        )
        for kk in range(per_chunk):
            i = j * per_chunk + kk
            for s in range(SLOTS):
                part = p_s[kk * half : kk * half + ROWS, s * TV : s * TV + TV]
                sbuf[s, i] = jnp.concatenate([part, ext_s[s, i]], axis=0).astype(BF)

    def unit(s, to):
        return sbuf.at[s, pl.ds(lax.rem(to + NX, NX) * ny, ny)]

    def x_copy(s, which):
        sign = 1 if s % 2 == 0 else -1
        ahead = lax.rem(x + sign + NX, NX) * ny + y
        behind = lax.rem(x - sign + NX, NX) * ny + y
        src, dst, to = (
            (lambda: unit(s, x + 2), relay_in, ahead),
            (lambda: unit(s, x - sign), from_one, behind),
            (lambda: relay_out.at[s], from_two, ahead),
        )[which]
        return remote(src(), dst.at[s], x_send.at[s, which], x_recv.at[s, which], to, gene)

    def y_copy(s, d):
        to = lax.rem(y + d, ny)
        return remote(
            yout.at[s, to], yin.at[s, ny - d], y_send.at[s], y_recv.at[s], x * ny + to, gene
        )

    def relay(s):
        sign = 1 if s % 2 == 0 else -1
        x_copy(s, 0).wait_recv()
        to = lax.rem(x + sign + NX, NX) * ny

        @pl.loop(0, ny)
        def _(b):
            relay_out[s, b] = (relay_in[s, b].astype(F32) + sbuf[s, to + b].astype(F32)).astype(BF)

        x_copy(s, 2).start()

    def over_x(s, b):
        return (
            sbuf[s, x * ny + b].astype(F32)
            + from_one[s, b].astype(F32)
            + from_two[s, b].astype(F32)
        )

    def gather_x(s):
        x_copy(s, 1).wait_recv()
        x_copy(s, 2).wait_recv()

        @pl.loop(0, ny)
        def _(b):
            yout[s, b] = over_x(s, b).astype(BF)

        @pl.loop(1, ny)
        def _(d):
            y_copy(s, d).start()

    for s in range(SLOTS):
        x_copy(s, 0).start()
        x_copy(s, 1).start()
    relay(0)
    relay(1)
    gather_x(0)
    relay(2)
    gather_x(1)
    relay(3)
    gather_x(2)
    gather_x(3)

    vrow = call_s[lax.div(ind, per_chunk)].astype(F32)[24:32]
    vrow = jnp.broadcast_to(vrow[0:1] + vrow[1:2] + vrow[2:3], (8, TV))
    var = vrow
    for kk in range(1, per_chunk):
        var = jnp.where(lax.rem(ind, per_chunk) == kk, pltpu.roll(vrow, TV - kk * half, 1), var)
    var = var[0:1, 0:ROWS]
    fin_s[...] = jnp.zeros_like(fin_s)
    for s in range(SLOTS):
        got = yin.at[s, pl.ds(1, ny - 1)]
        remote(got, got, y_send.at[s], y_recv.at[s], ind, gene).wait_recv()
        whole = over_x(s, y)
        for d in range(1, ny):
            whole = whole + yin[s, d].astype(F32)
        score = whole[0:ROWS]
        w = jnp.broadcast_to(weight[:, s * TV : s * TV + TV], (8, TV))
        burden = dot(w, score, "nt", HIGHEST)[0:1]
        skat = dot(w * w, score * score, "nt", HIGHEST)[0:1]
        b_den = 1.0 + whole[60:61, 0:ROWS] + whole[61:62, 0:ROWS]
        k_den = 1.0 + whole[62:63, 0:ROWS] + whole[63:64, 0:ROWS]
        fin_s[s : s + 1, 0:ROWS] = burden / jnp.sqrt(b_den * var)
        fin_s[4 + s : 5 + s, 0:ROWS] = skat / (k_den * var)
        up = 4 * (s // 2)
        left = TV + TV * (s % 2)
        fin_s[up : up + 4, left : left + TV] = whole[56:60] * (1.0 / n_total)

    @pl.loop(1, ng)
    def _(d):
        remote(fin_s, fall.at[ng - d], f_send, f_recv, ind, lax.rem(gene + d, ng)).start()

    fall[0] = fin_s[...]
    got = fall.at[pl.ds(1, ng - 1)]
    remote(got, got, f_send, f_recv, ind, gene).wait_recv()
    flat = fall[...].reshape(ng * 8, 3 * TV)
    stats = dot(pick[0:8], flat[:, 0:TV], "nn", HIGHEST)
    bz_ref[...] = stats[0:2, 0:half]
    sq_ref[...] = stats[2:4, 0:half]
    cov_out = dot(pick[8:16], flat[:, TV : 2 * TV], "nn", HIGHEST) + dot(
        pick[16:24], flat[:, 2 * TV :], "nn", HIGHEST
    )
    cv_ref[0] = cov_out[0:4]
    cv_ref[1] = cov_out[4:8]

    for step in range(1, nz // 2 + 1):
        for way, q in moves(step):
            ring(way, step, q).wait_send()
            across(way, step, q).wait_send()
    own_copy.wait_send()

    @pl.when(ind < units)
    def _():
        got = stat_s.at[pl.ds(0, units - 1)]
        remote(got, got, rs_send, rs_recv, ind, gene).wait_send()
        got = part_s.at[pl.ds(1, ni - 1)]
        remote(got, got, ag_send, ag_recv, ind, gene).wait_send()

    @pl.when(ind >= units)
    def _():
        remote(stat_s, stat_s, rs_send, rs_recv, ind, gene).wait_send()

    got = call_s.at[pl.ds(0, ng - 1)]
    remote(got, got, c_send, c_recv, ind, gene).wait_send()
    for s in range(SLOTS):
        for which in range(3):
            x_copy(s, which).wait_send()
        got = yout.at[s, pl.ds(0, ny - 1)]
        remote(got, got, y_send.at[s], y_recv.at[s], ind, gene).wait_send()
    got = fall.at[pl.ds(1, ng - 1)]
    remote(got, got, f_send, f_recv, ind, gene).wait_send()


def selections(home, length, me, ng):
    total = home.shape[1]
    owned = total // ng
    g_row, g_col = iota((total, total), 0), iota((total, total), 1)
    same = g_row == g_col

    def column(row):
        return jnp.sum(jnp.where(same, row, 0), axis=1, keepdims=True)

    home_col, len_col = column(home), column(length)
    before = jnp.where((home == home_col) & (g_col < g_row), 1, 0)
    rank = jnp.sum(before, axis=1, keepdims=True)
    gene_id = iota((total, 1), 0)

    def chosen(where, value):
        return jnp.sum(jnp.where(where, value, 0), axis=0, keepdims=True)

    variant = iota((1, TV), 1)
    live = [
        jnp.where(variant < chosen((home_col == me) & (rank == s), len_col), 1.0, 0.0)
        for s in range(SLOTS)
    ]
    mask = jnp.concatenate(live, axis=1)
    far = home_col - me
    far = jnp.where(far < 0, far + ng, far)
    here = [chosen(gene_id == me * owned + o, far) for o in range(owned)]
    slot = [chosen(gene_id == me * owned + o, rank) for o in range(owned)]
    r, c = iota((24, ng * 8), 0), iota((24, ng * 8), 1)
    first = jnp.where(r < 8, r % 2, (r - 8) % 8 // 4) == 0
    at = jnp.where(first, here[0], here[1])
    s = jnp.where(first, slot[0], slot[1])
    upper = jnp.where(s < 2, 0, 1)
    stat_col = at * 8 + jnp.where(r < 2, s, 4 + s)
    cov_col = at * 8 + upper * 4 + (r - 8) % 4
    cov_on = (s - upper * 2) == (r - 8) // 8
    hit = jnp.where(
        r < 8,
        jnp.where((c == stat_col) & (r < 4), 1.0, 0.0),
        jnp.where((c == cov_col) & cov_on, 1.0, 0.0),
    )
    return mask, hit


def per_device(genotypes, covariates, proteins, gene_device, tile_len):
    ni, ng = lax.axis_size("ind"), lax.axis_size("gene")
    rows, pt = proteins.shape
    lanes = SLOTS * TV
    half = pt * ng // ni
    owned = gene_device.shape[0] // ng
    units = TILES if ni >= TILES else 6
    tall_unit = TILES // units * 8
    ny, nz = ni // NX, ng // 2
    vmem = pl.BlockSpec(memory_space=pltpu.VMEM)
    dma = pltpu.SemaphoreType.DMA
    unit = (SLOTS, ny, BLOCK, TV)
    scratch = [
        pltpu.VMEM((rows, lanes), jnp.int32),
        pltpu.VMEM((rows, lanes), BF),
        pltpu.VMEM((rows, lanes), BF),
        pltpu.VMEM((32, rows), F32),
        pltpu.VMEM((96, rows), BF),
        pltpu.VMEM((rows, 256), BF),
        pltpu.VMEM((ng, 2, pt, rows // 2), BF),
        pltpu.VMEM((units, tall_unit, TV), F32),
        pltpu.VMEM((ni, tall_unit, TV), F32),
        pltpu.VMEM((tall_unit, TV), F32),
        pltpu.VMEM((units, tall_unit, TV), F32),
        pltpu.VMEM((ng, 32, TV), BF),
        pltpu.VMEM((SLOTS, ni, 8, TV), F32),
        pltpu.VMEM((112, lanes), F32),
        pltpu.VMEM((SLOTS, ni, BLOCK, TV), BF),
        pltpu.VMEM(unit, BF),
        pltpu.VMEM(unit, BF),
        pltpu.VMEM(unit, BF),
        pltpu.VMEM(unit, BF),
        pltpu.VMEM(unit, BF),
        pltpu.VMEM(unit, BF),
        pltpu.VMEM((8, 3 * TV), F32),
        pltpu.VMEM((ng, 8, 3 * TV), F32),
        dma,
        dma((2, nz // 2, 2)), dma((2, nz // 2, 2)),
        dma((2, nz // 2, 2)), dma((2, nz // 2, 2)),
        dma, dma, dma, dma, dma, dma, dma, dma,
        dma((SLOTS, 3)), dma((SLOTS, 3)),
        dma((SLOTS,)), dma((SLOTS,)),
        dma, dma,
    ]
    return pl.pallas_call(
        functools.partial(kernel, ni, ng, half, units),
        out_shape=(
            jax.ShapeDtypeStruct((owned, half), F32),
            jax.ShapeDtypeStruct((owned, half), F32),
            jax.ShapeDtypeStruct((owned, COV_ROWS, TV), F32),
        ),
        in_specs=[pl.BlockSpec(memory_space=pl.ANY), vmem, vmem, vmem, vmem],
        out_specs=(vmem, vmem, vmem),
        scratch_shapes=scratch,
        compiler_params=pltpu.CompilerParams(
            collective_id=0, has_side_effects=True, vmem_limit_bytes=66_000_000
        ),
    )(genotypes, covariates, proteins.T, gene_device[None, :], tile_len[None, :])


def solution(mesh):
    return jax.shard_map(
        per_device,
        mesh=mesh,
        in_specs=(P("ind", "gene"), P(None, "ind"), P("ind", "gene"), P(), P()),
        out_specs=(P("gene", "ind"), P("gene", "ind"), P("gene", "ind", None)),
        check_vma=False,
    )
```

```python
import functools

import jax
import jax.numpy as jnp
from jax import lax
from jax.experimental import pallas as pl
from jax.experimental.pallas import tpu as pltpu
from jax.sharding import PartitionSpec as P

COV = 20
WIDTH = COV + 1
TV = 128
SLOTS = 4
NX = 4
ROWS = 56
BLOCK = 64
PAIR = 2
COV_ROWS = 4
TILES = 18

BF = jnp.bfloat16
F32 = jnp.float32
HIGHEST = lax.Precision.HIGHEST
MESH = pl.DeviceIdType.MESH


def dot(a, b, form="nn", precision=None):
    dims = {"nn": ((1,), (0,)), "nt": ((1,), (1,)), "tn": ((0,), (0,))}[form]
    return lax.dot_general(a, b, (dims, ((), ())), precision=precision, preferred_element_type=F32)


def split3(v):
    hi = v.astype(BF).astype(F32)
    rest = v - hi
    mid = rest.astype(BF).astype(F32)
    return hi, mid, (rest - mid).astype(BF).astype(F32)


def iota(shape, dim):
    return lax.broadcasted_iota(jnp.int32, shape, dim)


def kernel(
    ni, ng, half, units,
    geno_ref, cov_ref, prot_ref, home_ref, len_ref,
    bz_ref, sq_ref, cv_ref,
    g_s, gb_s, gr_s, d_s, dst_s, dct_s, tall, stat_s, part_s, psum_s, total_s, call_s,
    ext_s, kx_all, p_s, sbuf, relay_in, relay_out, from_one, from_two, yout, yin, fin_s, fall,
    load_sem, t_send, t_recv, pair_send, pair_recv, own_send, own_recv,
    rs_send, rs_recv, ag_send, ag_recv, c_send, c_recv, x_send, x_recv, y_send, y_recv,
    k_send, k_recv, f_send, f_recv,
):
    ind, gene = lax.axis_index("ind"), lax.axis_index("gene")
    ny, nz = ni // NX, ng // 2
    x, y = lax.div(ind, ny), lax.rem(ind, ny)
    z, core = lax.div(gene, 2), lax.rem(gene, 2)
    pt, rows = prot_ref.shape
    half_rows = rows // 2
    per_chunk = ni // ng
    padded = per_chunk * ROWS
    unit_rows = ny * ROWS
    n_total = rows * ni
    lanes = SLOTS * TV
    per_unit = TILES // units

    def remote(src, dst, send, recv, i, g):
        return pltpu.make_async_remote_copy(
            src_ref=src, dst_ref=dst, send_sem=send, recv_sem=recv,
            device_id=(i, g), device_id_type=MESH,
        )

    load = pltpu.make_async_copy(geno_ref, g_s, load_sem)
    load.start()
    barrier = pltpu.get_barrier_semaphore()

    @pl.loop(1, ni)
    def _(d):
        pl.semaphore_signal(
            barrier, inc=1, device_id=(lax.rem(ind + d, ni), gene), device_id_type=MESH
        )

    @pl.loop(1, ng)
    def _(d):
        pl.semaphore_signal(
            barrier, inc=1, device_id=(ind, lax.rem(gene + d, ng)), device_id_type=MESH
        )

    spread_r, spread_c = iota((padded, pt), 0), iota((padded, pt), 1)
    spread = spread_r - spread_r // ROWS * (ROWS - half) == spread_c
    spread = jnp.where(spread & (spread_r % ROWS < half), 1.0, 0.0).astype(BF)
    tall_own = dot(spread, prot_ref[...]).astype(BF)
    own_rows = pl.ds(pl.multiple_of(gene * padded, padded), padded)
    tall[0, own_rows, :] = tall_own[:, :half_rows]
    tall[1, own_rows, :] = tall_own[:, half_rows:]
    mask, pick = selections(home_ref[...], len_ref[...], gene, ng)
    pl.semaphore_wait(barrier, ni + ng - 2)

    def chunk_of(way, step):
        sign = 1 if way == 0 else -1
        chunk = lax.rem(z - sign * step + 2 * nz, nz) * 2 + core
        return pl.ds(pl.multiple_of(chunk * padded, padded), padded)

    def ring(way, step, q):
        sign = 1 if way == 0 else -1
        block = tall.at[q, chunk_of(way, step - 1)]
        target = lax.rem(z + sign + nz, nz) * 2 + core
        return remote(
            block, block, t_send.at[way, step - 1, q], t_recv.at[way, step - 1, q], ind, target
        )

    def across(way, step, q):
        block = tall.at[q, chunk_of(way, step)]
        return remote(
            block, block, pair_send.at[way, step - 1, q], pair_recv.at[way, step - 1, q],
            ind, z * 2 + 1 - core,
        )

    def moves(step):
        if step < nz // 2:
            return [(way, q) for q in range(2) for way in range(2)]
        return [(0, 0), (1, 1)]

    def own_copy(q):
        block = tall.at[q, own_rows]
        return remote(block, block, own_send.at[q], own_recv.at[q], ind, z * 2 + 1 - core)

    for way, q in moves(1):
        ring(way, 1, q).start()
    for q in range(2):
        own_copy(q).start()

    def forward(step, half_of):
        if step > nz // 2:
            return
        for way, q in moves(step):
            if q == half_of:
                ring(way, step, q).wait_recv()
                if step < nz // 2 and (way, q) in moves(step + 1):
                    ring(way, step + 1, q).start()
                across(way, step, q).start()

    d_s[...] = jnp.zeros_like(d_s)
    d_s[0:1, :] = jnp.ones((1, rows), F32)
    d_s[1 : 1 + COV, :] = cov_ref[...]
    design = d_s[...]
    d1, d2, d3 = split3(design)
    dst_s[...] = jnp.concatenate([d1, d2, d3], axis=0).astype(BF)
    load.wait()
    step_rows = min(128, rows)

    @pl.loop(0, rows // step_rows)
    def _(b):
        at = pl.ds(pl.multiple_of(b * step_rows, step_rows), step_rows)
        gb_s[at, :] = (g_s[at, :].astype(F32) * mask).astype(BF)

    wide = dot(dst_s[...], gb_s[...])
    dg = wide[0:32] + wide[32:64] + wide[64:96]
    narrow = dot(dst_s[...], tall_own, "nt")
    dt = narrow[0:32] + narrow[32:64] + narrow[64:96]
    square = jnp.square(tall_own.astype(F32))
    sq_hi = square.astype(BF)
    sq_lo = (square - sq_hi.astype(F32)).astype(BF)
    ones = jnp.ones((16, rows), BF)
    t2 = dot(ones, sq_hi, "nt") + dot(ones, sq_lo, "nt")
    dt = dt[0:24] + jnp.where(iota((24, padded), 0) == WIDTH, t2[0:1], 0.0)
    gram = dot(design, design, "nt", HIGHEST)
    stat_s[...] = jnp.zeros_like(stat_s)
    for r in range(3):
        sub = slice(8 * r, 8 * r + 8)
        for c in range(SLOTS):
            k = r * SLOTS + c
            at = slice(8 * (k % per_unit), 8 * (k % per_unit) + 8)
            stat_s[k // per_unit, at, :] = dg[sub, TV * c : TV * c + TV]
        k = 12 + r
        at = slice(8 * (k % per_unit), 8 * (k % per_unit) + 8)
        stat_s[k // per_unit, at, 0:padded] = dt[sub]
        k = 15 + r
        at = slice(8 * (k % per_unit), 8 * (k % per_unit) + 8)
        stat_s[k // per_unit, at, 0:32] = gram[sub]

    def to_owner(t):
        return remote(
            stat_s.at[t], part_s.at[lax.rem(ind - t + ni, ni)], rs_send, rs_recv, t, gene
        )

    @pl.loop(0, units)
    def _(t):
        @pl.when(t != ind)
        def _():
            to_owner(t).start()

    forward(1, 0)
    dcat = jnp.concatenate([d1, d2, d3, d1, d2, d1, jnp.zeros((64, rows), F32)], axis=0)
    dct_s[...] = jnp.transpose(dcat).astype(BF)
    forward(1, 1)
    forward(2, 0)

    @pl.when(ind < units)
    def _():
        part_s[0] = stat_s[ind]
        got = part_s.at[pl.ds(1, ni - 1)]
        remote(got, got, rs_send, rs_recv, ind, gene).wait_recv()
        subtotal = jnp.sum(part_s[...], axis=0)
        psum_s[...] = subtotal
        total_s[ind] = subtotal

        @pl.loop(1, ni)
        def _(d):
            remote(
                psum_s, total_s.at[ind], ag_send, ag_recv, lax.rem(ind + d, ni), gene
            ).start()

    forward(2, 1)
    forward(3, 0)
    forward(3, 1)

    @pl.when(ind < units)
    def _():
        got = total_s.at[pl.ds(0, units - 1)]
        remote(got, got, ag_send, ag_recv, ind, gene).wait_recv()

    @pl.when(ind >= units)
    def _():
        remote(total_s, total_s, ag_send, ag_recv, ind, gene).wait_recv()

    def tile(k):
        return total_s[k // per_unit, 8 * (k % per_unit) : 8 * (k % per_unit) + 8, :]

    cross_geno = jnp.concatenate(
        [jnp.concatenate([tile(r * SLOTS + c) for c in range(SLOTS)], axis=1) for r in range(3)],
        axis=0,
    )
    traits = jnp.concatenate([tile(12 + r) for r in range(3)], axis=0)
    gram_sum = jnp.concatenate([tile(15 + r) for r in range(3)], axis=0)
    t2_sum = traits[WIDTH : WIDTH + 1]
    cross_traits = jnp.where(iota((24, TV), 0) < WIDTH, traits, 0.0)
    work = jnp.concatenate([gram_sum, cross_geno, cross_traits], axis=1)
    row_id = iota(work.shape, 0)
    for k in range(WIDTH):
        pivot = work[k : k + 1] / work[k : k + 1, k : k + 1]
        work = jnp.where(row_id == k, pivot, work - work[:, k : k + 1] * pivot)
    geno_coef = work[:, TV : TV + lanes]
    trait_coef = work[:, TV + lanes :]
    variance = (t2_sum - jnp.sum(cross_traits * trait_coef, axis=0, keepdims=True)) / (
        n_total - WIDTH
    ) + 1e-05
    v1, v2, v3 = split3(variance)
    sub8 = iota((8, TV), 0)
    tail = jnp.where(sub8 == 0, v1, jnp.where(sub8 == 1, v2, jnp.where(sub8 == 2, v3, 0.0)))
    call_s[gene] = jnp.concatenate([trait_coef, tail], axis=0).astype(BF)

    @pl.loop(1, ng)
    def _(d):
        remote(
            call_s.at[gene], call_s.at[gene], c_send, c_recv, ind, lax.rem(gene + d, ng)
        ).start()

    forward(4, 0)
    forward(4, 1)
    base = 1.0 - cross_geno[0:1] / (2.0 * n_total)
    b2 = base * base
    b4 = b2 * b2
    b8 = b4 * b4
    weight = 25.0 * (b8 * b8 * b8) * mask

    c1, c2, c3 = split3(jnp.concatenate([geno_coef, jnp.zeros((8, lanes), F32)], axis=0))
    rcat = jnp.concatenate([c1, c1, c1, c2, c2, c3, jnp.zeros((64, lanes), F32)], axis=0).astype(BF)

    @pl.loop(0, rows // step_rows)
    def _(b):
        at = pl.ds(pl.multiple_of(b * step_rows, step_rows), step_rows)
        gr_s[at, :] = (gb_s[at, :].astype(F32) - dot(dct_s[at, :], rcat)).astype(BF)

    wide = dot(dst_s[...], gr_s[...])
    h1, h2, h3 = split3(wide[0:32] + wide[32:64] + wide[64:96])
    hcat = jnp.concatenate([h1, h2, h3], axis=0).astype(BF)

    sel_r, sel_c = iota((ni * 8, TV), 0), iota((ni * 8, TV), 1)
    sub = lax.rem(sel_r, 8) - 8 + COV_ROWS
    sel = jnp.where((sub >= 0) & (sel_c == lax.div(sel_r, 8) * COV_ROWS + sub), 1.0, 0.0)
    sel = sel.astype(BF)
    diag = iota((TV, TV), 0) == iota((TV, TV), 1)
    extra = jnp.zeros((8, TV), F32)
    for s in range(SLOTS):
        cols = slice(s * TV, s * TV + TV)
        tile_r = gr_s[:, cols]
        cov_s = dot(tile_r, tile_r, "tn")
        w = weight[:, cols]
        wc = dot(jnp.broadcast_to(w, (8, TV)), cov_s, "nn", HIGHEST)
        burden = jnp.sum(wc[0:1] * w, axis=1, keepdims=True)
        dosage = jnp.sum(jnp.where(diag, cov_s, 0.0), axis=0, keepdims=True)
        skat = jnp.sum(dosage * w * w, axis=1, keepdims=True)
        extra = jnp.where(sub8 == s, burden, jnp.where(sub8 == SLOTS + s, skat, extra))
        ext_s[s] = dot(sel, cov_s.astype(BF)).reshape(ni, 8, TV)
    kx_all[0] = extra

    @pl.loop(1, ni)
    def _(d):
        remote(
            kx_all.at[0], kx_all.at[ni - d], k_send, k_recv, lax.rem(ind + d, ni), gene
        ).start()

    got = call_s.at[pl.ds(0, ng - 1)]
    remote(got, got, c_send, c_recv, ind, gene).wait_recv()
    for q in range(2):
        own_copy(q).wait_recv()
    for step in range(1, nz // 2 + 1):
        for way, q in moves(step):
            across(way, step, q).wait_recv()

    def part_of_scores(pair):
        cols = slice(pair * PAIR * TV, (pair + 1) * PAIR * TV)
        chunks = unit_rows // padded

        @pl.loop(0, NX)
        def _(u):
            at = pl.ds(pl.multiple_of(u * unit_rows, unit_rows), unit_rows)
            p_s[...] = dot(tall[0, at, :], gr_s[0:half_rows, cols]) + dot(
                tall[1, at, :], gr_s[half_rows:, cols]
            )
            for c in range(chunks):
                cj = call_s[u * chunks + c]
                fix = dot(jnp.concatenate([cj, cj, cj], axis=0), hcat[:, cols], "tn")
                p_s[c * padded : (c + 1) * padded, :] -= fix[0:padded]
            for k in range(PAIR):
                s = pair * PAIR + k
                lanes_k = slice(k * TV, k * TV + TV)
                for b in range(ny):
                    last = slice(b * ROWS + ROWS - 8, b * ROWS + ROWS)
                    p_s[last, lanes_k] += ext_s[s, u * ny + b]
                sbuf[s, u] = p_s[:, lanes_k].astype(BF)

    def unit(s, to):
        return sbuf.at[s, lax.rem(to + NX, NX)]

    def x_copy(s, which):
        sign = 1 if s % 2 == 0 else -1
        ahead = lax.rem(x + sign + NX, NX) * ny + y
        behind = lax.rem(x - sign + NX, NX) * ny + y
        src, dst, to = (
            (lambda: unit(s, x + 2), relay_in, ahead),
            (lambda: unit(s, x - sign), from_one, behind),
            (lambda: relay_out.at[s], from_two, ahead),
        )[which]
        return remote(src(), dst.at[s], x_send.at[s, which], x_recv.at[s, which], to, gene)

    def y_copy(s, d):
        to = lax.rem(y + d, ny)
        return remote(
            yout.at[s, to], yin.at[s, ny - d], y_send.at[s], y_recv.at[s], x * ny + to, gene
        )

    def start(s):
        x_copy(s, 0).start()
        x_copy(s, 1).start()

    both = 2 * ROWS

    def relay(s):
        sign = 1 if s % 2 == 0 else -1
        x_copy(s, 0).wait_recv()
        to = lax.rem(x + sign + NX, NX)

        @pl.loop(0, ny // 2)
        def _(b):
            at = pl.ds(pl.multiple_of(b * both, both), both)
            relay_out[s, at, :] = (
                relay_in[s, at, :].astype(F32) + sbuf[s, to, at, :].astype(F32)
            ).astype(BF)

        x_copy(s, 2).start()

    def over_x(s, b):
        at = pl.ds(pl.multiple_of(b * both, both), both)
        return (
            sbuf[s, x, at, :].astype(F32)
            + from_one[s, at, :].astype(F32)
            + from_two[s, at, :].astype(F32)
        )

    def gather_x(s):
        x_copy(s, 1).wait_recv()
        x_copy(s, 2).wait_recv()
        pad = jnp.zeros((BLOCK - ROWS, TV), F32)

        @pl.loop(0, ny // 2)
        def _(b):
            v = over_x(s, b)
            yout[s, 2 * b] = jnp.concatenate([v[:ROWS], pad], axis=0).astype(BF)
            yout[s, 2 * b + 1] = jnp.concatenate([v[ROWS:], pad], axis=0).astype(BF)

        @pl.loop(1, ny)
        def _(d):
            y_copy(s, d).start()

    part_of_scores(0)
    start(0)
    start(1)
    part_of_scores(1)
    relay(0)
    start(2)
    relay(1)
    start(3)
    gather_x(0)
    relay(2)
    gather_x(1)
    relay(3)
    gather_x(2)
    gather_x(3)

    vrow = call_s[lax.div(ind, per_chunk)].astype(F32)[24:32]
    vrow = jnp.broadcast_to(vrow[0:1] + vrow[1:2] + vrow[2:3], (8, TV))
    var = vrow
    for kk in range(1, per_chunk):
        var = jnp.where(lax.rem(ind, per_chunk) == kk, pltpu.roll(vrow, TV - kk * ROWS, 1), var)
    var = var[0:1, 0:ROWS]
    got = kx_all.at[pl.ds(1, ni - 1)]
    remote(got, got, k_send, k_recv, ind, gene).wait_recv()
    dens = 1.0 + jnp.sum(kx_all[...], axis=0)
    fin_s[...] = jnp.zeros_like(fin_s)
    for s in range(SLOTS):
        got = yin.at[s, pl.ds(1, ny - 1)]
        remote(got, got, y_send.at[s], y_recv.at[s], ind, gene).wait_recv()
        v = over_x(s, lax.div(y, 2))
        whole = jnp.where(lax.rem(y, 2) == 0, v[:ROWS], v[ROWS:])
        for d in range(1, ny):
            whole = whole + yin[s, d].astype(F32)[:ROWS]
        w = jnp.broadcast_to(weight[:, s * TV : s * TV + TV], (8, TV))
        burden = dot(w, whole, "nt", HIGHEST)[0:1]
        skat = dot(w * w, whole * whole, "nt", HIGHEST)[0:1]
        b_den = dens[s : s + 1, 0:ROWS]
        k_den = dens[SLOTS + s : SLOTS + s + 1, 0:ROWS]
        fin_s[s : s + 1, 0:ROWS] = burden / jnp.sqrt(b_den * var)
        fin_s[4 + s : 5 + s, 0:ROWS] = skat / (k_den * var)
        up = 4 * (s // 2)
        left = TV + TV * (s % 2)
        fin_s[up : up + 4, left : left + TV] = whole[ROWS - COV_ROWS : ROWS] * (1.0 / n_total)

    @pl.loop(1, ng)
    def _(d):
        remote(fin_s, fall.at[ng - d], f_send, f_recv, ind, lax.rem(gene + d, ng)).start()

    fall[0] = fin_s[...]
    got = fall.at[pl.ds(1, ng - 1)]
    remote(got, got, f_send, f_recv, ind, gene).wait_recv()
    flat = fall[...].reshape(ng * 8, 3 * TV)
    stats = dot(pick[0:8], flat[:, 0:TV], "nn", HIGHEST)
    bz_ref[...] = stats[0:2, 0:half]
    sq_ref[...] = stats[2:4, 0:half]
    cov_out = dot(pick[8:16], flat[:, TV : 2 * TV], "nn", HIGHEST) + dot(
        pick[16:24], flat[:, 2 * TV :], "nn", HIGHEST
    )
    cv_ref[0] = cov_out[0:4]
    cv_ref[1] = cov_out[4:8]

    for step in range(1, nz // 2 + 1):
        for way, q in moves(step):
            ring(way, step, q).wait_send()
            across(way, step, q).wait_send()
    for q in range(2):
        own_copy(q).wait_send()

    @pl.when(ind < units)
    def _():
        got = stat_s.at[pl.ds(0, units - 1)]
        remote(got, got, rs_send, rs_recv, ind, gene).wait_send()
        got = part_s.at[pl.ds(1, ni - 1)]
        remote(got, got, ag_send, ag_recv, ind, gene).wait_send()

    @pl.when(ind >= units)
    def _():
        remote(stat_s, stat_s, rs_send, rs_recv, ind, gene).wait_send()

    got = call_s.at[pl.ds(0, ng - 1)]
    remote(got, got, c_send, c_recv, ind, gene).wait_send()
    got = kx_all.at[pl.ds(1, ni - 1)]
    remote(got, got, k_send, k_recv, ind, gene).wait_send()
    for s in range(SLOTS):
        for which in range(3):
            x_copy(s, which).wait_send()
        got = yout.at[s, pl.ds(0, ny - 1)]
        remote(got, got, y_send.at[s], y_recv.at[s], ind, gene).wait_send()
    got = fall.at[pl.ds(1, ng - 1)]
    remote(got, got, f_send, f_recv, ind, gene).wait_send()


def selections(home, length, me, ng):
    total = home.shape[1]
    owned = total // ng
    g_row, g_col = iota((total, total), 0), iota((total, total), 1)
    same = g_row == g_col

    def column(row):
        return jnp.sum(jnp.where(same, row, 0), axis=1, keepdims=True)

    home_col, len_col = column(home), column(length)
    before = jnp.where((home == home_col) & (g_col < g_row), 1, 0)
    rank = jnp.sum(before, axis=1, keepdims=True)
    gene_id = iota((total, 1), 0)

    def chosen(where, value):
        return jnp.sum(jnp.where(where, value, 0), axis=0, keepdims=True)

    variant = iota((1, TV), 1)
    live = [
        jnp.where(variant < chosen((home_col == me) & (rank == s), len_col), 1.0, 0.0)
        for s in range(SLOTS)
    ]
    mask = jnp.concatenate(live, axis=1)
    far = home_col - me
    far = jnp.where(far < 0, far + ng, far)
    here = [chosen(gene_id == me * owned + o, far) for o in range(owned)]
    slot = [chosen(gene_id == me * owned + o, rank) for o in range(owned)]
    r, c = iota((24, ng * 8), 0), iota((24, ng * 8), 1)
    first = jnp.where(r < 8, r % 2, (r - 8) % 8 // 4) == 0
    at = jnp.where(first, here[0], here[1])
    s = jnp.where(first, slot[0], slot[1])
    upper = jnp.where(s < 2, 0, 1)
    stat_col = at * 8 + jnp.where(r < 2, s, 4 + s)
    cov_col = at * 8 + upper * 4 + (r - 8) % 4
    cov_on = (s - upper * 2) == (r - 8) // 8
    hit = jnp.where(
        r < 8,
        jnp.where((c == stat_col) & (r < 4), 1.0, 0.0),
        jnp.where((c == cov_col) & cov_on, 1.0, 0.0),
    )
    return mask, hit


def per_device(genotypes, covariates, proteins, gene_device, tile_len):
    ni, ng = lax.axis_size("ind"), lax.axis_size("gene")
    rows, pt = proteins.shape
    lanes = SLOTS * TV
    half = pt * ng // ni
    owned = gene_device.shape[0] // ng
    units = TILES if ni >= TILES else 6
    tall_unit = TILES // units * 8
    ny, nz = ni // NX, ng // 2
    vmem = pl.BlockSpec(memory_space=pltpu.VMEM)
    dma = pltpu.SemaphoreType.DMA
    unit = (SLOTS, ny * ROWS, TV)
    block = (SLOTS, ny, BLOCK, TV)
    padded = ni // ng * ROWS
    scratch = [
        pltpu.VMEM((rows, lanes), jnp.int32),
        pltpu.VMEM((rows, lanes), BF),
        pltpu.VMEM((rows, lanes), BF),
        pltpu.VMEM((32, rows), F32),
        pltpu.VMEM((96, rows), BF),
        pltpu.VMEM((rows, 256), BF),
        pltpu.VMEM((2, ng * padded, rows // 2), BF),
        pltpu.VMEM((units, tall_unit, TV), F32),
        pltpu.VMEM((ni, tall_unit, TV), F32),
        pltpu.VMEM((tall_unit, TV), F32),
        pltpu.VMEM((units, tall_unit, TV), F32),
        pltpu.VMEM((ng, 32, TV), BF),
        pltpu.VMEM((SLOTS, ni, 8, TV), F32),
        pltpu.VMEM((ni, 8, TV), F32),
        pltpu.VMEM((ny * ROWS, PAIR * TV), F32),
        pltpu.VMEM((SLOTS, NX, ny * ROWS, TV), BF),
        pltpu.VMEM(unit, BF),
        pltpu.VMEM(unit, BF),
        pltpu.VMEM(unit, BF),
        pltpu.VMEM(unit, BF),
        pltpu.VMEM(block, BF),
        pltpu.VMEM(block, BF),
        pltpu.VMEM((8, 3 * TV), F32),
        pltpu.VMEM((ng, 8, 3 * TV), F32),
        dma,
        dma((2, nz // 2, 2)), dma((2, nz // 2, 2)),
        dma((2, nz // 2, 2)), dma((2, nz // 2, 2)),
        dma((2,)), dma((2,)), dma, dma, dma, dma, dma, dma,
        dma((SLOTS, 3)), dma((SLOTS, 3)),
        dma((SLOTS,)), dma((SLOTS,)),
        dma, dma, dma, dma,
    ]
    return pl.pallas_call(
        functools.partial(kernel, ni, ng, half, units),
        out_shape=(
            jax.ShapeDtypeStruct((owned, half), F32),
            jax.ShapeDtypeStruct((owned, half), F32),
            jax.ShapeDtypeStruct((owned, COV_ROWS, TV), F32),
        ),
        in_specs=[pl.BlockSpec(memory_space=pl.ANY), vmem, vmem, vmem, vmem],
        out_specs=(vmem, vmem, vmem),
        scratch_shapes=scratch,
        compiler_params=pltpu.CompilerParams(
            collective_id=0, has_side_effects=True, vmem_limit_bytes=66_000_000
        ),
    )(genotypes, covariates, proteins.T, gene_device[None, :], tile_len[None, :])


def solution(mesh):
    return jax.shard_map(
        per_device,
        mesh=mesh,
        in_specs=(P("ind", "gene"), P(None, "ind"), P("ind", "gene"), P(), P()),
        out_specs=(P("gene", "ind"), P("gene", "ind"), P("gene", "ind", None)),
        check_vma=False,
    )
```

```python
import functools

import jax
import jax.numpy as jnp
from jax import lax
from jax.experimental import pallas as pl
from jax.experimental.pallas import tpu as pltpu
from jax.sharding import PartitionSpec as P

COV = 20
WIDTH = COV + 1
TV = 128
SLOTS = 4
NX = 4
ROWS = 56
PAIR = 2
COV_ROWS = 4
TILES = 18

BF = jnp.bfloat16
F32 = jnp.float32
HIGHEST = lax.Precision.HIGHEST
MESH = pl.DeviceIdType.MESH


def dot(a, b, form="nn", precision=None):
    dims = {"nn": ((1,), (0,)), "nt": ((1,), (1,)), "tn": ((0,), (0,))}[form]
    return lax.dot_general(a, b, (dims, ((), ())), precision=precision, preferred_element_type=F32)


def split3(v):
    hi = v.astype(BF).astype(F32)
    rest = v - hi
    mid = rest.astype(BF).astype(F32)
    return hi, mid, (rest - mid).astype(BF).astype(F32)


def iota(shape, dim):
    return lax.broadcasted_iota(jnp.int32, shape, dim)


def kernel(
    ni, ng, half, units,
    geno_ref, cov_ref, prot_ref, home_ref, len_ref,
    bz_ref, sq_ref, cv_ref,
    g_s, gb_s, gr_s, d_s, dst_s, dct_s, tall, stat_s, part_s, psum_s, total_s, call_s,
    ext_s, kx_all, p_s, sbuf, relay_in, relay_out, from_one, from_two, yout, yin, fin_s, fall,
    load_sem, t_send, t_recv, pair_send, pair_recv, own_send, own_recv,
    rs_send, rs_recv, ag_send, ag_recv, c_send, c_recv, x_send, x_recv, y_send, y_recv,
    k_send, k_recv, f_send, f_recv,
):
    ind, gene = lax.axis_index("ind"), lax.axis_index("gene")
    ny, nz = ni // NX, ng // 2
    x, y = lax.div(ind, ny), lax.rem(ind, ny)
    z, core = lax.div(gene, 2), lax.rem(gene, 2)
    pt, rows = prot_ref.shape
    half_rows = rows // 2
    per_chunk = ni // ng
    padded = per_chunk * ROWS
    unit_rows = ny * ROWS
    n_total = rows * ni
    lanes = SLOTS * TV
    per_unit = TILES // units

    def remote(src, dst, send, recv, i, g):
        return pltpu.make_async_remote_copy(
            src_ref=src, dst_ref=dst, send_sem=send, recv_sem=recv,
            device_id=(i, g), device_id_type=MESH,
        )

    load = pltpu.make_async_copy(geno_ref, g_s, load_sem)
    load.start()
    barrier = pltpu.get_barrier_semaphore()

    @pl.loop(1, ni)
    def _(d):
        pl.semaphore_signal(
            barrier, inc=1, device_id=(lax.rem(ind + d, ni), gene), device_id_type=MESH
        )

    @pl.loop(1, ng)
    def _(d):
        pl.semaphore_signal(
            barrier, inc=1, device_id=(ind, lax.rem(gene + d, ng)), device_id_type=MESH
        )

    pl.semaphore_wait(barrier, ni + ng - 2)

    def chunk_of(way, step):
        sign = 1 if way == 0 else -1
        chunk = lax.rem(z - sign * step + 2 * nz, nz) * 2 + core
        return pl.ds(pl.multiple_of(chunk * padded, padded), pt)

    def ring(way, step, q):
        sign = 1 if way == 0 else -1
        block = tall.at[q, chunk_of(way, step - 1)]
        source = block if step > 1 else prot_ref.at[:, pl.ds(q * half_rows, half_rows)]
        target = lax.rem(z + sign + nz, nz) * 2 + core
        return remote(
            source, block, t_send.at[way, step - 1, q], t_recv.at[way, step - 1, q], ind, target
        )

    def across(way, step, q):
        block = tall.at[q, chunk_of(way, step)]
        return remote(
            block, block, pair_send.at[way, step - 1, q], pair_recv.at[way, step - 1, q],
            ind, z * 2 + 1 - core,
        )

    def moves(step):
        if step < nz // 2:
            return [(way, q) for q in range(2) for way in range(2)]
        return [(0, 0), (1, 1)]

    own_rows = pl.ds(pl.multiple_of(gene * padded, padded), pt)

    def own_copy(q):
        source = prot_ref.at[:, pl.ds(q * half_rows, half_rows)]
        block = tall.at[q, own_rows]
        return remote(source, block, own_send.at[q], own_recv.at[q], ind, z * 2 + 1 - core)

    for way, q in moves(1):
        ring(way, 1, q).start()
    for q in range(2):
        own_copy(q).start()
    tall_own = prot_ref[...]
    tall[0, own_rows, :] = tall_own[:, :half_rows]
    tall[1, own_rows, :] = tall_own[:, half_rows:]
    mask, pick = selections(home_ref[...], len_ref[...], gene, ng)

    def forward(step, half_of):
        if step > nz // 2:
            return
        for way, q in moves(step):
            if q == half_of:
                ring(way, step, q).wait_recv()
                if step < nz // 2 and (way, q) in moves(step + 1):
                    ring(way, step + 1, q).start()
                across(way, step, q).start()

    d_s[...] = jnp.zeros_like(d_s)
    d_s[0:1, :] = jnp.ones((1, rows), F32)
    d_s[1 : 1 + COV, :] = cov_ref[...]
    design = d_s[...]
    d1, d2, d3 = split3(design)
    dst_s[...] = jnp.concatenate([d1, d2, d3], axis=0).astype(BF)
    load.wait()
    step_rows = min(128, rows)

    @pl.loop(0, rows // step_rows)
    def _(b):
        at = pl.ds(pl.multiple_of(b * step_rows, step_rows), step_rows)
        gb_s[at, :] = (g_s[at, :].astype(F32) * mask).astype(BF)

    wide = dot(dst_s[...], gb_s[...])
    dg = wide[0:32] + wide[32:64] + wide[64:96]
    narrow = dot(dst_s[...], tall_own, "nt")
    dt = narrow[0:32] + narrow[32:64] + narrow[64:96]
    square = jnp.square(tall_own.astype(F32))
    sq_hi = square.astype(BF)
    sq_lo = (square - sq_hi.astype(F32)).astype(BF)
    ones = jnp.ones((16, rows), BF)
    t2 = dot(ones, sq_hi, "nt") + dot(ones, sq_lo, "nt")
    dt = dt[0:24] + jnp.where(iota((24, pt), 0) == WIDTH, t2[0:1], 0.0)
    gram = dot(design, design, "nt", HIGHEST)
    stat_s[...] = jnp.zeros_like(stat_s)
    for r in range(3):
        sub = slice(8 * r, 8 * r + 8)
        for c in range(SLOTS):
            k = r * SLOTS + c
            at = slice(8 * (k % per_unit), 8 * (k % per_unit) + 8)
            stat_s[k // per_unit, at, :] = dg[sub, TV * c : TV * c + TV]
        k = 12 + r
        at = slice(8 * (k % per_unit), 8 * (k % per_unit) + 8)
        stat_s[k // per_unit, at, 0:pt] = dt[sub]
        k = 15 + r
        at = slice(8 * (k % per_unit), 8 * (k % per_unit) + 8)
        stat_s[k // per_unit, at, 0:32] = gram[sub]

    def to_owner(t):
        return remote(
            stat_s.at[t], part_s.at[lax.rem(ind - t + ni, ni)], rs_send, rs_recv, t, gene
        )

    @pl.loop(0, units)
    def _(t):
        @pl.when(t != ind)
        def _():
            to_owner(t).start()

    forward(1, 0)
    dcat = jnp.concatenate([d1, d2, d3, d1, d2, d1, jnp.zeros((64, rows), F32)], axis=0)
    dct_s[...] = jnp.transpose(dcat).astype(BF)
    forward(1, 1)
    forward(2, 0)

    @pl.when(ind < units)
    def _():
        part_s[0] = stat_s[ind]
        got = part_s.at[pl.ds(1, ni - 1)]
        remote(got, got, rs_send, rs_recv, ind, gene).wait_recv()
        subtotal = jnp.sum(part_s[...], axis=0)
        psum_s[...] = subtotal
        total_s[ind] = subtotal

        @pl.loop(1, ni)
        def _(d):
            remote(
                psum_s, total_s.at[ind], ag_send, ag_recv, lax.rem(ind + d, ni), gene
            ).start()

    forward(2, 1)
    forward(3, 0)
    forward(3, 1)

    @pl.when(ind < units)
    def _():
        got = total_s.at[pl.ds(0, units - 1)]
        remote(got, got, ag_send, ag_recv, ind, gene).wait_recv()

    @pl.when(ind >= units)
    def _():
        remote(total_s, total_s, ag_send, ag_recv, ind, gene).wait_recv()

    def tile(k):
        return total_s[k // per_unit, 8 * (k % per_unit) : 8 * (k % per_unit) + 8, :]

    cross_geno = jnp.concatenate(
        [jnp.concatenate([tile(r * SLOTS + c) for c in range(SLOTS)], axis=1) for r in range(3)],
        axis=0,
    )
    traits = jnp.concatenate([tile(12 + r) for r in range(3)], axis=0)
    gram_sum = jnp.concatenate([tile(15 + r) for r in range(3)], axis=0)
    t2_sum = traits[WIDTH : WIDTH + 1]
    cross_traits = jnp.where(iota((24, TV), 0) < WIDTH, traits, 0.0)
    work = jnp.concatenate([gram_sum, cross_geno, cross_traits], axis=1)
    row_id = iota(work.shape, 0)
    for k in range(WIDTH):
        pivot = work[k : k + 1] / work[k : k + 1, k : k + 1]
        work = jnp.where(row_id == k, pivot, work - work[:, k : k + 1] * pivot)
    geno_coef = work[:, TV : TV + lanes]
    trait_coef = work[:, TV + lanes :]
    variance = (t2_sum - jnp.sum(cross_traits * trait_coef, axis=0, keepdims=True)) / (
        n_total - WIDTH
    ) + 1e-05
    v1, v2, v3 = split3(variance)
    sub8 = iota((8, TV), 0)
    tail = jnp.where(sub8 == 0, v1, jnp.where(sub8 == 1, v2, jnp.where(sub8 == 2, v3, 0.0)))
    call_s[gene] = jnp.concatenate([trait_coef, tail], axis=0).astype(BF)

    @pl.loop(1, ng)
    def _(d):
        remote(
            call_s.at[gene], call_s.at[gene], c_send, c_recv, ind, lax.rem(gene + d, ng)
        ).start()

    forward(4, 0)
    forward(4, 1)
    base = 1.0 - cross_geno[0:1] / (2.0 * n_total)
    b2 = base * base
    b4 = b2 * b2
    b8 = b4 * b4
    weight = 25.0 * (b8 * b8 * b8) * mask

    c1, c2, c3 = split3(jnp.concatenate([geno_coef, jnp.zeros((8, lanes), F32)], axis=0))
    rcat = jnp.concatenate([c1, c1, c1, c2, c2, c3, jnp.zeros((64, lanes), F32)], axis=0).astype(BF)

    @pl.loop(0, rows // step_rows)
    def _(b):
        at = pl.ds(pl.multiple_of(b * step_rows, step_rows), step_rows)
        gr_s[at, :] = (gb_s[at, :].astype(F32) - dot(dct_s[at, :], rcat)).astype(BF)

    wide = dot(dst_s[...], gr_s[...])
    h1, h2, h3 = split3(wide[0:32] + wide[32:64] + wide[64:96])
    hcat = jnp.concatenate([h1, h2, h3], axis=0).astype(BF)

    sel_r, sel_c = iota((ni * 8, TV), 0), iota((ni * 8, TV), 1)
    sub = lax.rem(sel_r, 8) - 8 + COV_ROWS
    sel = jnp.where((sub >= 0) & (sel_c == lax.div(sel_r, 8) * COV_ROWS + sub), 1.0, 0.0)
    sel = sel.astype(BF)
    diag = iota((TV, TV), 0) == iota((TV, TV), 1)
    extra = jnp.zeros((8, TV), F32)
    for s in range(SLOTS):
        cols = slice(s * TV, s * TV + TV)
        tile_r = gr_s[:, cols]
        cov_s = dot(tile_r, tile_r, "tn")
        w = weight[:, cols]
        wc = dot(jnp.broadcast_to(w, (8, TV)), cov_s, "nn", HIGHEST)
        burden = jnp.sum(wc[0:1] * w, axis=1, keepdims=True)
        dosage = jnp.sum(jnp.where(diag, cov_s, 0.0), axis=0, keepdims=True)
        skat = jnp.sum(dosage * w * w, axis=1, keepdims=True)
        extra = jnp.where(sub8 == s, burden, jnp.where(sub8 == SLOTS + s, skat, extra))
        ext_s[s] = dot(sel, cov_s.astype(BF)).reshape(ni, 8, TV)
    kx_all[0] = extra

    @pl.loop(1, ni)
    def _(d):
        remote(
            kx_all.at[0], kx_all.at[ni - d], k_send, k_recv, lax.rem(ind + d, ni), gene
        ).start()

    got = call_s.at[pl.ds(0, ng - 1)]
    remote(got, got, c_send, c_recv, ind, gene).wait_recv()
    for q in range(2):
        own_copy(q).wait_recv()
    for step in range(1, nz // 2 + 1):
        for way, q in moves(step):
            across(way, step, q).wait_recv()

    def part_of_scores(pair):
        cols = slice(pair * PAIR * TV, (pair + 1) * PAIR * TV)
        chunks = unit_rows // padded

        @pl.loop(0, NX)
        def _(u):
            at = pl.ds(pl.multiple_of(u * unit_rows, unit_rows), unit_rows)
            p_s[...] = dot(tall[0, at, :], gr_s[0:half_rows, cols]) + dot(
                tall[1, at, :], gr_s[half_rows:, cols]
            )
            for c in range(chunks):
                cj = call_s[u * chunks + c]
                fix = dot(jnp.concatenate([cj, cj, cj], axis=0), hcat[:, cols], "tn")
                p_s[c * padded : (c + 1) * padded, :] -= fix[0:padded]
            for k in range(PAIR):
                s = pair * PAIR + k
                lanes_k = slice(k * TV, k * TV + TV)
                blocks = []
                for b in range(ny):
                    low = b // per_chunk * padded + b % per_chunk * half
                    blocks.append(p_s[low : low + ROWS - 8, lanes_k])
                    end = p_s[low + ROWS - 8 : low + ROWS, lanes_k]
                    blocks.append(jnp.where(sub8 < 8 - COV_ROWS, end, ext_s[s, u * ny + b]))
                sbuf[s, u] = jnp.concatenate(blocks, axis=0).astype(BF)

    def unit(s, to):
        return sbuf.at[s, lax.rem(to + NX, NX)]

    def x_copy(s, which):
        sign = 1 if s % 2 == 0 else -1
        ahead = lax.rem(x + sign + NX, NX) * ny + y
        behind = lax.rem(x - sign + NX, NX) * ny + y
        src, dst, to = (
            (lambda: unit(s, x + 2), relay_in, ahead),
            (lambda: unit(s, x - sign), from_one, behind),
            (lambda: relay_out.at[s], from_two, ahead),
        )[which]
        return remote(src(), dst.at[s], x_send.at[s, which], x_recv.at[s, which], to, gene)

    def y_copy(s, d):
        to = lax.rem(y + d, ny)
        return remote(
            yout.at[s, to], yin.at[s, ny - d], y_send.at[s], y_recv.at[s], x * ny + to, gene
        )

    def start(s):
        x_copy(s, 0).start()
        x_copy(s, 1).start()

    both = 2 * ROWS

    def relay(s):
        sign = 1 if s % 2 == 0 else -1
        x_copy(s, 0).wait_recv()
        to = lax.rem(x + sign + NX, NX)

        @pl.loop(0, ny // 2)
        def _(b):
            at = pl.ds(pl.multiple_of(b * both, both), both)
            relay_out[s, at, :] = (
                relay_in[s, at, :].astype(F32) + sbuf[s, to, at, :].astype(F32)
            ).astype(BF)

        x_copy(s, 2).start()

    def over_x(s, b):
        at = pl.ds(pl.multiple_of(b * both, both), both)
        return (
            sbuf[s, x, at, :].astype(F32)
            + from_one[s, at, :].astype(F32)
            + from_two[s, at, :].astype(F32)
        )

    def gather_x(s):
        x_copy(s, 1).wait_recv()
        x_copy(s, 2).wait_recv()

        @pl.loop(0, ny // 2)
        def _(b):
            v = over_x(s, b)
            yout[s, 2 * b] = v[:ROWS].astype(BF)
            yout[s, 2 * b + 1] = v[ROWS:].astype(BF)

        @pl.loop(1, ny)
        def _(d):
            y_copy(s, d).start()

    def finish(s, var, dens):
        got = yin.at[s, pl.ds(1, ny - 1)]
        remote(got, got, y_send.at[s], y_recv.at[s], ind, gene).wait_recv()
        v = over_x(s, lax.div(y, 2))
        whole = jnp.where(lax.rem(y, 2) == 0, v[:ROWS], v[ROWS:])
        for d in range(1, ny):
            whole = whole + yin[s, d].astype(F32)
        w = jnp.broadcast_to(weight[:, s * TV : s * TV + TV], (8, TV))
        burden = dot(w, whole, "nt", HIGHEST)[0:1]
        skat = dot(w * w, whole * whole, "nt", HIGHEST)[0:1]
        fin_s[s, 0:COV_ROWS, :] = whole[ROWS - COV_ROWS : ROWS] * (1.0 / n_total)
        fin_s[s, 4:5, 0:ROWS] = burden / jnp.sqrt(dens[s : s + 1, 0:ROWS] * var)
        fin_s[s, 5:6, 0:ROWS] = skat / (dens[SLOTS + s : SLOTS + s + 1, 0:ROWS] * var)
        fall[s, 0] = fin_s[s]

        @pl.loop(1, ng)
        def _(d):
            remote(
                fin_s.at[s], fall.at[s, ng - d], f_send.at[s], f_recv.at[s],
                ind, lax.rem(gene + d, ng),
            ).start()

    part_of_scores(0)
    start(0)
    start(1)
    part_of_scores(1)
    relay(0)
    start(2)
    relay(1)
    start(3)
    fin_s[...] = jnp.zeros_like(fin_s)
    vrow = call_s[lax.div(ind, per_chunk)].astype(F32)[24:32]
    vrow = jnp.broadcast_to(vrow[0:1] + vrow[1:2] + vrow[2:3], (8, TV))
    var = vrow
    for kk in range(1, per_chunk):
        var = jnp.where(lax.rem(ind, per_chunk) == kk, pltpu.roll(vrow, TV - kk * half, 1), var)
    var = var[0:1, 0:ROWS]
    got = kx_all.at[pl.ds(1, ni - 1)]
    remote(got, got, k_send, k_recv, ind, gene).wait_recv()
    dens = 1.0 + jnp.sum(kx_all[...], axis=0)
    gather_x(0)
    relay(2)
    gather_x(1)
    relay(3)
    gather_x(2)
    finish(0, var, dens)
    gather_x(3)
    for s in range(1, SLOTS):
        finish(s, var, dens)
    for s in range(SLOTS):
        got = fall.at[s, pl.ds(1, ng - 1)]
        remote(got, got, f_send.at[s], f_recv.at[s], ind, gene).wait_recv()
    mine = dot(pick, fall[...].reshape(SLOTS * ng * 8, TV), "nn", HIGHEST)
    bz_ref[...] = mine[0:2, 0:half]
    sq_ref[...] = mine[2:4, 0:half]
    cv_ref[0] = mine[8:12]
    cv_ref[1] = mine[12:16]

    for step in range(1, nz // 2 + 1):
        for way, q in moves(step):
            ring(way, step, q).wait_send()
            across(way, step, q).wait_send()
    for q in range(2):
        own_copy(q).wait_send()

    @pl.when(ind < units)
    def _():
        got = stat_s.at[pl.ds(0, units - 1)]
        remote(got, got, rs_send, rs_recv, ind, gene).wait_send()
        got = part_s.at[pl.ds(1, ni - 1)]
        remote(got, got, ag_send, ag_recv, ind, gene).wait_send()

    @pl.when(ind >= units)
    def _():
        remote(stat_s, stat_s, rs_send, rs_recv, ind, gene).wait_send()

    got = call_s.at[pl.ds(0, ng - 1)]
    remote(got, got, c_send, c_recv, ind, gene).wait_send()
    got = kx_all.at[pl.ds(1, ni - 1)]
    remote(got, got, k_send, k_recv, ind, gene).wait_send()
    for s in range(SLOTS):
        for which in range(3):
            x_copy(s, which).wait_send()
        got = yout.at[s, pl.ds(0, ny - 1)]
        remote(got, got, y_send.at[s], y_recv.at[s], ind, gene).wait_send()
    for s in range(SLOTS):
        got = fall.at[s, pl.ds(1, ng - 1)]
        remote(got, got, f_send.at[s], f_recv.at[s], ind, gene).wait_send()


def selections(home, length, me, ng):
    total = home.shape[1]
    owned = total // ng
    g_row, g_col = iota((total, total), 0), iota((total, total), 1)
    same = g_row == g_col

    def column(row):
        return jnp.sum(jnp.where(same, row, 0), axis=1, keepdims=True)

    home_col, len_col = column(home), column(length)
    before = jnp.where((home == home_col) & (g_col < g_row), 1, 0)
    rank = jnp.sum(before, axis=1, keepdims=True)
    gene_id = iota((total, 1), 0)

    def chosen(where, value):
        return jnp.sum(jnp.where(where, value, 0), axis=0, keepdims=True)

    variant = iota((1, TV), 1)
    live = [
        jnp.where(variant < chosen((home_col == me) & (rank == s), len_col), 1.0, 0.0)
        for s in range(SLOTS)
    ]
    mask = jnp.concatenate(live, axis=1)
    far = home_col - me
    far = jnp.where(far < 0, far + ng, far)
    here = [chosen(gene_id == me * owned + o, far) for o in range(owned)]
    slot = [chosen(gene_id == me * owned + o, rank) for o in range(owned)]
    r, c = iota((16, SLOTS * ng * 8), 0), iota((16, SLOTS * ng * 8), 1)
    first = jnp.where(r < 8, r % 2, (r - 8) // 4) == 0
    at = jnp.where(first, here[0], here[1])
    s = jnp.where(first, slot[0], slot[1])
    line = jnp.where(r < 8, jnp.where(r < 2, 4, 5), r % 4)
    hit = (c == (s * ng + at) * 8 + line) & ((r < 4) | (r >= 8))
    return mask, jnp.where(hit, 1.0, 0.0)


def per_device(genotypes, covariates, proteins, gene_device, tile_len):
    ni, ng = lax.axis_size("ind"), lax.axis_size("gene")
    rows, pt = proteins.shape
    lanes = SLOTS * TV
    half = pt * ng // ni
    owned = gene_device.shape[0] // ng
    units = TILES if ni >= TILES else 6
    tall_unit = TILES // units * 8
    ny, nz = ni // NX, ng // 2
    vmem = pl.BlockSpec(memory_space=pltpu.VMEM)
    dma = pltpu.SemaphoreType.DMA
    unit = (SLOTS, ny * ROWS, TV)
    block = (SLOTS, ny, ROWS, TV)
    padded = ni // ng * ROWS
    scratch = [
        pltpu.VMEM((rows, lanes), jnp.int32),
        pltpu.VMEM((rows, lanes), BF),
        pltpu.VMEM((rows, lanes), BF),
        pltpu.VMEM((32, rows), F32),
        pltpu.VMEM((96, rows), BF),
        pltpu.VMEM((rows, 256), BF),
        pltpu.VMEM((2, ng * padded, rows // 2), BF),
        pltpu.VMEM((units, tall_unit, TV), F32),
        pltpu.VMEM((ni, tall_unit, TV), F32),
        pltpu.VMEM((tall_unit, TV), F32),
        pltpu.VMEM((units, tall_unit, TV), F32),
        pltpu.VMEM((ng, 32, TV), BF),
        pltpu.VMEM((SLOTS, ni, 8, TV), F32),
        pltpu.VMEM((ni, 8, TV), F32),
        pltpu.VMEM((ny * ROWS, PAIR * TV), F32),
        pltpu.VMEM((SLOTS, NX, ny * ROWS, TV), BF),
        pltpu.VMEM(unit, BF),
        pltpu.VMEM(unit, BF),
        pltpu.VMEM(unit, BF),
        pltpu.VMEM(unit, BF),
        pltpu.VMEM(block, BF),
        pltpu.VMEM(block, BF),
        pltpu.VMEM((SLOTS, 8, TV), F32),
        pltpu.VMEM((SLOTS, ng, 8, TV), F32),
        dma,
        dma((2, nz // 2, 2)), dma((2, nz // 2, 2)),
        dma((2, nz // 2, 2)), dma((2, nz // 2, 2)),
        dma((2,)), dma((2,)), dma, dma, dma, dma, dma, dma,
        dma((SLOTS, 3)), dma((SLOTS, 3)),
        dma((SLOTS,)), dma((SLOTS,)),
        dma, dma, dma((SLOTS,)), dma((SLOTS,)),
    ]
    return pl.pallas_call(
        functools.partial(kernel, ni, ng, half, units),
        out_shape=(
            jax.ShapeDtypeStruct((owned, half), F32),
            jax.ShapeDtypeStruct((owned, half), F32),
            jax.ShapeDtypeStruct((owned, COV_ROWS, TV), F32),
        ),
        in_specs=[pl.BlockSpec(memory_space=pl.ANY), vmem, vmem, vmem, vmem],
        out_specs=(vmem, vmem, vmem),
        scratch_shapes=scratch,
        compiler_params=pltpu.CompilerParams(
            collective_id=0, has_side_effects=True, vmem_limit_bytes=66_000_000
        ),
    )(genotypes, covariates, proteins.T, gene_device[None, :], tile_len[None, :])


def solution(mesh):
    return jax.shard_map(
        per_device,
        mesh=mesh,
        in_specs=(P("ind", "gene"), P(None, "ind"), P("ind", "gene"), P(), P()),
        out_specs=(P("gene", "ind"), P("gene", "ind"), P("gene", "ind", None)),
        check_vma=False,
    )
```

```python
import functools

import jax
import jax.numpy as jnp
from jax import lax
from jax.experimental import pallas as pl
from jax.experimental.pallas import tpu as pltpu
from jax.sharding import PartitionSpec as P

COV = 20
WIDTH = COV + 1
TV = 128
SLOTS = 4
NX = 4
ROWS = 56
PAIR = 2
X_FIRST = 3
COV_ROWS = 4
TILES = 18

BF = jnp.bfloat16
F32 = jnp.float32
HIGHEST = lax.Precision.HIGHEST
MESH = pl.DeviceIdType.MESH


def dot(a, b, form="nn", precision=None):
    dims = {"nn": ((1,), (0,)), "nt": ((1,), (1,)), "tn": ((0,), (0,))}[form]
    return lax.dot_general(a, b, (dims, ((), ())), precision=precision, preferred_element_type=F32)


def split3(v):
    hi = v.astype(BF).astype(F32)
    rest = v - hi
    mid = rest.astype(BF).astype(F32)
    return hi, mid, (rest - mid).astype(BF).astype(F32)


def iota(shape, dim):
    return lax.broadcasted_iota(jnp.int32, shape, dim)


def kernel(
    ni, ng, half, units,
    geno_ref, cov_ref, prot_ref, home_ref, len_ref,
    bz_ref, sq_ref, cv_ref,
    s3, r_in, r_out, l_in, l_out, x3_out, x3_in, g_s, gb_s, gr_s, d_s, dst_s, dct_s, tall, stat_s, part_s, psum_s, total_s, call_s,
    ext_s, kx_all, p_s, sbuf, relay_in, relay_out, from_one, from_two, yout, yin, fin_s, fall,
    r_send, r_recv, l_send, l_recv, x3_send, x3_recv, load_sem, t_send, t_recv, pair_send, pair_recv, own_send, own_recv,
    rs_send, rs_recv, ag_send, ag_recv, c_send, c_recv, x_send, x_recv, y_send, y_recv,
    k_send, k_recv, f_send, f_recv,
):
    ind, gene = lax.axis_index("ind"), lax.axis_index("gene")
    ny, nz = ni // NX, ng // 2
    x, y = lax.div(ind, ny), lax.rem(ind, ny)
    z, core = lax.div(gene, 2), lax.rem(gene, 2)
    pt, rows = prot_ref.shape
    half_rows = rows // 2
    per_chunk = ni // ng
    padded = per_chunk * ROWS
    unit_rows = ny * ROWS
    n_total = rows * ni
    lanes = SLOTS * TV
    per_unit = TILES // units

    def remote(src, dst, send, recv, i, g):
        return pltpu.make_async_remote_copy(
            src_ref=src, dst_ref=dst, send_sem=send, recv_sem=recv,
            device_id=(i, g), device_id_type=MESH,
        )

    load = pltpu.make_async_copy(geno_ref, g_s, load_sem)
    load.start()
    barrier = pltpu.get_barrier_semaphore()

    @pl.loop(1, ni)
    def _(d):
        pl.semaphore_signal(
            barrier, inc=1, device_id=(lax.rem(ind + d, ni), gene), device_id_type=MESH
        )

    @pl.loop(1, ng)
    def _(d):
        pl.semaphore_signal(
            barrier, inc=1, device_id=(ind, lax.rem(gene + d, ng)), device_id_type=MESH
        )

    pl.semaphore_wait(barrier, ni + ng - 2)

    def chunk_of(way, step):
        sign = 1 if way == 0 else -1
        chunk = lax.rem(z - sign * step + 2 * nz, nz) * 2 + core
        return pl.ds(pl.multiple_of(chunk * padded, padded), pt)

    def ring(way, step, q):
        sign = 1 if way == 0 else -1
        block = tall.at[q, chunk_of(way, step - 1)]
        source = block if step > 1 else prot_ref.at[:, pl.ds(q * half_rows, half_rows)]
        target = lax.rem(z + sign + nz, nz) * 2 + core
        return remote(
            source, block, t_send.at[way, step - 1, q], t_recv.at[way, step - 1, q], ind, target
        )

    def across(way, step, q):
        block = tall.at[q, chunk_of(way, step)]
        return remote(
            block, block, pair_send.at[way, step - 1, q], pair_recv.at[way, step - 1, q],
            ind, z * 2 + 1 - core,
        )

    def moves(step):
        if step < nz // 2:
            return [(way, q) for q in range(2) for way in range(2)]
        return [(0, 0), (1, 1)]

    own_rows = pl.ds(pl.multiple_of(gene * padded, padded), pt)

    def own_copy(q):
        source = prot_ref.at[:, pl.ds(q * half_rows, half_rows)]
        block = tall.at[q, own_rows]
        return remote(source, block, own_send.at[q], own_recv.at[q], ind, z * 2 + 1 - core)

    for way, q in moves(1):
        ring(way, 1, q).start()
    for q in range(2):
        own_copy(q).start()
    tall_own = prot_ref[...]
    tall[0, own_rows, :] = tall_own[:, :half_rows]
    tall[1, own_rows, :] = tall_own[:, half_rows:]
    mask, pick = selections(home_ref[...], len_ref[...], gene, ng)

    def forward(step, half_of):
        if step > nz // 2:
            return
        for way, q in moves(step):
            if q == half_of:
                ring(way, step, q).wait_recv()
                if step < nz // 2 and (way, q) in moves(step + 1):
                    ring(way, step + 1, q).start()
                across(way, step, q).start()

    d_s[...] = jnp.zeros_like(d_s)
    d_s[0:1, :] = jnp.ones((1, rows), F32)
    d_s[1 : 1 + COV, :] = cov_ref[...]
    design = d_s[...]
    d1, d2, d3 = split3(design)
    dst_s[...] = jnp.concatenate([d1, d2, d3], axis=0).astype(BF)
    load.wait()
    step_rows = min(128, rows)

    @pl.loop(0, rows // step_rows)
    def _(b):
        at = pl.ds(pl.multiple_of(b * step_rows, step_rows), step_rows)
        gb_s[at, :] = (g_s[at, :].astype(F32) * mask).astype(BF)

    wide = dot(dst_s[...], gb_s[...])
    dg = wide[0:32] + wide[32:64] + wide[64:96]
    narrow = dot(dst_s[...], tall_own, "nt")
    dt = narrow[0:32] + narrow[32:64] + narrow[64:96]
    square = jnp.square(tall_own.astype(F32))
    sq_hi = square.astype(BF)
    sq_lo = (square - sq_hi.astype(F32)).astype(BF)
    ones = jnp.ones((16, rows), BF)
    t2 = dot(ones, sq_hi, "nt") + dot(ones, sq_lo, "nt")
    dt = dt[0:24] + jnp.where(iota((24, pt), 0) == WIDTH, t2[0:1], 0.0)
    gram = dot(design, design, "nt", HIGHEST)
    stat_s[...] = jnp.zeros_like(stat_s)
    for r in range(3):
        sub = slice(8 * r, 8 * r + 8)
        for c in range(SLOTS):
            k = r * SLOTS + c
            at = slice(8 * (k % per_unit), 8 * (k % per_unit) + 8)
            stat_s[k // per_unit, at, :] = dg[sub, TV * c : TV * c + TV]
        k = 12 + r
        at = slice(8 * (k % per_unit), 8 * (k % per_unit) + 8)
        stat_s[k // per_unit, at, 0:pt] = dt[sub]
        k = 15 + r
        at = slice(8 * (k % per_unit), 8 * (k % per_unit) + 8)
        stat_s[k // per_unit, at, 0:32] = gram[sub]

    def to_owner(t):
        return remote(
            stat_s.at[t], part_s.at[lax.rem(ind - t + ni, ni)], rs_send, rs_recv, t, gene
        )

    @pl.loop(0, units)
    def _(t):
        @pl.when(t != ind)
        def _():
            to_owner(t).start()

    forward(1, 0)
    dcat = jnp.concatenate([d1, d2, d3, d1, d2, d1, jnp.zeros((64, rows), F32)], axis=0)
    dct_s[...] = jnp.transpose(dcat).astype(BF)
    forward(1, 1)
    forward(2, 0)

    @pl.when(ind < units)
    def _():
        part_s[0] = stat_s[ind]
        got = part_s.at[pl.ds(1, ni - 1)]
        remote(got, got, rs_send, rs_recv, ind, gene).wait_recv()
        subtotal = jnp.sum(part_s[...], axis=0)
        psum_s[...] = subtotal
        total_s[ind] = subtotal

        @pl.loop(1, ni)
        def _(d):
            remote(
                psum_s, total_s.at[ind], ag_send, ag_recv, lax.rem(ind + d, ni), gene
            ).start()

    forward(2, 1)
    forward(3, 0)
    forward(3, 1)

    @pl.when(ind < units)
    def _():
        got = total_s.at[pl.ds(0, units - 1)]
        remote(got, got, ag_send, ag_recv, ind, gene).wait_recv()

    @pl.when(ind >= units)
    def _():
        remote(total_s, total_s, ag_send, ag_recv, ind, gene).wait_recv()

    def tile(k):
        return total_s[k // per_unit, 8 * (k % per_unit) : 8 * (k % per_unit) + 8, :]

    cross_geno = jnp.concatenate(
        [jnp.concatenate([tile(r * SLOTS + c) for c in range(SLOTS)], axis=1) for r in range(3)],
        axis=0,
    )
    traits = jnp.concatenate([tile(12 + r) for r in range(3)], axis=0)
    gram_sum = jnp.concatenate([tile(15 + r) for r in range(3)], axis=0)
    t2_sum = traits[WIDTH : WIDTH + 1]
    cross_traits = jnp.where(iota((24, TV), 0) < WIDTH, traits, 0.0)
    work = jnp.concatenate([gram_sum, cross_geno, cross_traits], axis=1)
    row_id = iota(work.shape, 0)
    for k in range(WIDTH):
        pivot = work[k : k + 1] / work[k : k + 1, k : k + 1]
        work = jnp.where(row_id == k, pivot, work - work[:, k : k + 1] * pivot)
    geno_coef = work[:, TV : TV + lanes]
    trait_coef = work[:, TV + lanes :]
    variance = (t2_sum - jnp.sum(cross_traits * trait_coef, axis=0, keepdims=True)) / (
        n_total - WIDTH
    ) + 1e-05
    v1, v2, v3 = split3(variance)
    sub8 = iota((8, TV), 0)
    tail = jnp.where(sub8 == 0, v1, jnp.where(sub8 == 1, v2, jnp.where(sub8 == 2, v3, 0.0)))
    call_s[gene] = jnp.concatenate([trait_coef, tail], axis=0).astype(BF)

    @pl.loop(1, ng)
    def _(d):
        remote(
            call_s.at[gene], call_s.at[gene], c_send, c_recv, ind, lax.rem(gene + d, ng)
        ).start()

    forward(4, 0)
    forward(4, 1)
    base = 1.0 - cross_geno[0:1] / (2.0 * n_total)
    b2 = base * base
    b4 = b2 * b2
    b8 = b4 * b4
    weight = 25.0 * (b8 * b8 * b8) * mask

    c1, c2, c3 = split3(jnp.concatenate([geno_coef, jnp.zeros((8, lanes), F32)], axis=0))
    rcat = jnp.concatenate([c1, c1, c1, c2, c2, c3, jnp.zeros((64, lanes), F32)], axis=0).astype(BF)

    @pl.loop(0, rows // step_rows)
    def _(b):
        at = pl.ds(pl.multiple_of(b * step_rows, step_rows), step_rows)
        gr_s[at, :] = (gb_s[at, :].astype(F32) - dot(dct_s[at, :], rcat)).astype(BF)

    wide = dot(dst_s[...], gr_s[...])
    h1, h2, h3 = split3(wide[0:32] + wide[32:64] + wide[64:96])
    hcat = jnp.concatenate([h1, h2, h3], axis=0).astype(BF)

    sel_r, sel_c = iota((ni * 8, TV), 0), iota((ni * 8, TV), 1)
    sub = lax.rem(sel_r, 8) - 8 + COV_ROWS
    sel = jnp.where((sub >= 0) & (sel_c == lax.div(sel_r, 8) * COV_ROWS + sub), 1.0, 0.0)
    sel = sel.astype(BF)
    diag = iota((TV, TV), 0) == iota((TV, TV), 1)
    extra = jnp.zeros((8, TV), F32)
    for s in range(SLOTS):
        cols = slice(s * TV, s * TV + TV)
        tile_r = gr_s[:, cols]
        cov_s = dot(tile_r, tile_r, "tn")
        w = weight[:, cols]
        wc = dot(jnp.broadcast_to(w, (8, TV)), cov_s, "nn", HIGHEST)
        burden = jnp.sum(wc[0:1] * w, axis=1, keepdims=True)
        dosage = jnp.sum(jnp.where(diag, cov_s, 0.0), axis=0, keepdims=True)
        skat = jnp.sum(dosage * w * w, axis=1, keepdims=True)
        extra = jnp.where(sub8 == s, burden, jnp.where(sub8 == SLOTS + s, skat, extra))
        ext_s[s] = dot(sel, cov_s.astype(BF)).reshape(ni, 8, TV)
    kx_all[0] = extra

    @pl.loop(1, ni)
    def _(d):
        remote(
            kx_all.at[0], kx_all.at[ni - d], k_send, k_recv, lax.rem(ind + d, ni), gene
        ).start()

    got = call_s.at[pl.ds(0, ng - 1)]
    remote(got, got, c_send, c_recv, ind, gene).wait_recv()
    for q in range(2):
        own_copy(q).wait_recv()
    for step in range(1, nz // 2 + 1):
        for way, q in moves(step):
            across(way, step, q).wait_recv()

    def part_of_scores(pair):
        cols = slice(pair * PAIR * TV, (pair + 1) * PAIR * TV)
        chunks = unit_rows // padded

        @pl.loop(0, NX)
        def _(u):
            at = pl.ds(pl.multiple_of(u * unit_rows, unit_rows), unit_rows)
            p_s[...] = dot(tall[0, at, :], gr_s[0:half_rows, cols]) + dot(
                tall[1, at, :], gr_s[half_rows:, cols]
            )
            for c in range(chunks):
                cj = call_s[u * chunks + c]
                fix = dot(jnp.concatenate([cj, cj, cj], axis=0), hcat[:, cols], "tn")
                p_s[c * padded : (c + 1) * padded, :] -= fix[0:padded]
            for k in range(PAIR):
                s = pair * PAIR + k
                lanes_k = slice(k * TV, k * TV + TV)
                blocks = []
                for b in range(ny):
                    low = b // per_chunk * padded + b % per_chunk * half
                    blocks.append(p_s[low : low + ROWS - 8, lanes_k])
                    end = p_s[low + ROWS - 8 : low + ROWS, lanes_k]
                    blocks.append(jnp.where(sub8 < 8 - COV_ROWS, end, ext_s[s, u * ny + b]))
                if s < X_FIRST:
                    sbuf[s, u] = jnp.concatenate(blocks, axis=0).astype(BF)
                else:
                    for b in range(ny):
                        pair_of = jnp.concatenate(blocks[2 * b : 2 * b + 2], axis=0)
                        s3[b, u] = pair_of.astype(BF)

    def unit(s, to):
        return sbuf.at[s, lax.rem(to + NX, NX)]

    def x_copy(s, which):
        sign = 1 if s % 2 == 0 else -1
        ahead = lax.rem(x + sign + NX, NX) * ny + y
        behind = lax.rem(x - sign + NX, NX) * ny + y
        src, dst, to = (
            (lambda: unit(s, x + 2), relay_in, ahead),
            (lambda: unit(s, x - sign), from_one, behind),
            (lambda: relay_out.at[s], from_two, ahead),
        )[which]
        return remote(src(), dst.at[s], x_send.at[s, which], x_recv.at[s, which], to, gene)

    def y_copy(s, d):
        to = lax.rem(y + d, ny)
        return remote(
            yout.at[s, to], yin.at[s, ny - d], y_send.at[s], y_recv.at[s], x * ny + to, gene
        )

    def start(s):
        x_copy(s, 0).start()
        x_copy(s, 1).start()

    both = 2 * ROWS

    def relay(s):
        sign = 1 if s % 2 == 0 else -1
        x_copy(s, 0).wait_recv()
        to = lax.rem(x + sign + NX, NX)

        @pl.loop(0, ny // 2)
        def _(b):
            at = pl.ds(pl.multiple_of(b * both, both), both)
            relay_out[s, at, :] = (
                relay_in[s, at, :].astype(F32) + sbuf[s, to, at, :].astype(F32)
            ).astype(BF)

        x_copy(s, 2).start()

    def over_x(s, b):
        at = pl.ds(pl.multiple_of(b * both, both), both)
        return (
            sbuf[s, x, at, :].astype(F32)
            + from_one[s, at, :].astype(F32)
            + from_two[s, at, :].astype(F32)
        )

    def gather_x(s):
        x_copy(s, 1).wait_recv()
        x_copy(s, 2).wait_recv()

        @pl.loop(0, ny // 2)
        def _(b):
            v = over_x(s, b)
            yout[s, 2 * b] = v[:ROWS].astype(BF)
            yout[s, 2 * b + 1] = v[ROWS:].astype(BF)

        @pl.loop(1, ny)
        def _(d):
            y_copy(s, d).start()

    far = ny // 2

    def at_y(k):
        return lax.rem(y + k + ny, ny)

    def y_right(t):
        source = s3.at[at_y(far)] if t == 1 else r_out.at[t - 2]
        to = x * ny + at_y(1)
        return remote(source, r_in.at[t - 1], r_send.at[t - 1], r_recv.at[t - 1], to, gene)

    def y_left(t):
        source = s3.at[at_y(1 - far)] if t == 1 else l_out.at[t - 2]
        to = x * ny + at_y(-1)
        return remote(source, l_in.at[t - 1], l_send.at[t - 1], l_recv.at[t - 1], to, gene)

    def y_step(t):
        if t <= far:
            if t > 1:
                y_right(t - 1).wait_recv()
                r_out[t - 2] = (
                    r_in[t - 2].astype(F32) + s3[at_y(far + 1 - t)].astype(F32)
                ).astype(BF)
            y_right(t).start()
        if t < far:
            if t > 1:
                y_left(t - 1).wait_recv()
                l_out[t - 2] = (
                    l_in[t - 2].astype(F32) + s3[at_y(t - far)].astype(F32)
                ).astype(BF)
            y_left(t).start()

    def over_y(k):
        total = s3[y, k].astype(F32) + r_in[far - 1, k].astype(F32)
        return total + l_in[far - 2, k].astype(F32) if far > 1 else total

    def x3_copy(d):
        to = lax.rem(x + d, NX)
        return remote(x3_out.at[to], x3_in.at[NX - d], x3_send, x3_recv, to * ny + y, gene)

    def gather_y():
        y_right(far).wait_recv()
        if far > 1:
            y_left(far - 1).wait_recv()
        for k in range(NX):
            x3_out[k] = over_y(k).astype(BF)
        for d in range(1, NX):
            x3_copy(d).start()

    def whole_of(s):
        if s < X_FIRST:
            got = yin.at[s, pl.ds(1, ny - 1)]
            remote(got, got, y_send.at[s], y_recv.at[s], ind, gene).wait_recv()
            v = over_x(s, lax.div(y, 2))
            whole = jnp.where(lax.rem(y, 2) == 0, v[:ROWS], v[ROWS:])
            for d in range(1, ny):
                whole = whole + yin[s, d].astype(F32)
            return whole
        got = x3_in.at[pl.ds(1, NX - 1)]
        remote(got, got, x3_send, x3_recv, ind, gene).wait_recv()
        whole = over_y(x)
        for d in range(1, NX):
            whole = whole + x3_in[d].astype(F32)
        return whole

    def finish(s, var, dens):
        whole = whole_of(s)
        w = jnp.broadcast_to(weight[:, s * TV : s * TV + TV], (8, TV))
        burden = dot(w, whole, "nt", HIGHEST)[0:1]
        skat = dot(w * w, whole * whole, "nt", HIGHEST)[0:1]
        fin_s[s, 0:COV_ROWS, :] = whole[ROWS - COV_ROWS : ROWS] * (1.0 / n_total)
        fin_s[s, 4:5, 0:ROWS] = burden / jnp.sqrt(dens[s : s + 1, 0:ROWS] * var)
        fin_s[s, 5:6, 0:ROWS] = skat / (dens[SLOTS + s : SLOTS + s + 1, 0:ROWS] * var)
        fall[s, 0] = fin_s[s]

        @pl.loop(1, ng)
        def _(d):
            remote(
                fin_s.at[s], fall.at[s, ng - d], f_send.at[s], f_recv.at[s],
                ind, lax.rem(gene + d, ng),
            ).start()

    part_of_scores(1)
    y_step(1)
    start(2)
    part_of_scores(0)
    start(0)
    relay(2)
    y_step(2)
    start(1)
    fin_s[...] = jnp.zeros_like(fin_s)
    vrow = call_s[lax.div(ind, per_chunk)].astype(F32)[24:32]
    vrow = jnp.broadcast_to(vrow[0:1] + vrow[1:2] + vrow[2:3], (8, TV))
    var = vrow
    for kk in range(1, per_chunk):
        var = jnp.where(lax.rem(ind, per_chunk) == kk, pltpu.roll(vrow, TV - kk * half, 1), var)
    var = var[0:1, 0:ROWS]
    got = kx_all.at[pl.ds(1, ni - 1)]
    remote(got, got, k_send, k_recv, ind, gene).wait_recv()
    dens = 1.0 + jnp.sum(kx_all[...], axis=0)
    relay(0)
    y_step(3)
    gather_x(2)
    relay(1)
    y_step(4)
    gather_x(0)
    finish(2, var, dens)
    gather_y()
    gather_x(1)
    finish(0, var, dens)
    finish(3, var, dens)
    finish(1, var, dens)
    for s in range(SLOTS):
        got = fall.at[s, pl.ds(1, ng - 1)]
        remote(got, got, f_send.at[s], f_recv.at[s], ind, gene).wait_recv()
    mine = dot(pick, fall[...].reshape(SLOTS * ng * 8, TV), "nn", HIGHEST)
    bz_ref[...] = mine[0:2, 0:half]
    sq_ref[...] = mine[2:4, 0:half]
    cv_ref[0] = mine[8:12]
    cv_ref[1] = mine[12:16]

    for step in range(1, nz // 2 + 1):
        for way, q in moves(step):
            ring(way, step, q).wait_send()
            across(way, step, q).wait_send()
    for q in range(2):
        own_copy(q).wait_send()

    @pl.when(ind < units)
    def _():
        got = stat_s.at[pl.ds(0, units - 1)]
        remote(got, got, rs_send, rs_recv, ind, gene).wait_send()
        got = part_s.at[pl.ds(1, ni - 1)]
        remote(got, got, ag_send, ag_recv, ind, gene).wait_send()

    @pl.when(ind >= units)
    def _():
        remote(stat_s, stat_s, rs_send, rs_recv, ind, gene).wait_send()

    got = call_s.at[pl.ds(0, ng - 1)]
    remote(got, got, c_send, c_recv, ind, gene).wait_send()
    got = kx_all.at[pl.ds(1, ni - 1)]
    remote(got, got, k_send, k_recv, ind, gene).wait_send()
    for t in range(1, far + 1):
        y_right(t).wait_send()
        if t < far:
            y_left(t).wait_send()
    got = x3_in.at[pl.ds(1, NX - 1)]
    remote(got, got, x3_send, x3_recv, ind, gene).wait_send()
    for s in range(X_FIRST):
        for which in range(3):
            x_copy(s, which).wait_send()
        got = yout.at[s, pl.ds(0, ny - 1)]
        remote(got, got, y_send.at[s], y_recv.at[s], ind, gene).wait_send()
    for s in range(SLOTS):
        got = fall.at[s, pl.ds(1, ng - 1)]
        remote(got, got, f_send.at[s], f_recv.at[s], ind, gene).wait_send()


def selections(home, length, me, ng):
    total = home.shape[1]
    owned = total // ng
    g_row, g_col = iota((total, total), 0), iota((total, total), 1)
    same = g_row == g_col

    def column(row):
        return jnp.sum(jnp.where(same, row, 0), axis=1, keepdims=True)

    home_col, len_col = column(home), column(length)
    before = jnp.where((home == home_col) & (g_col < g_row), 1, 0)
    rank = jnp.sum(before, axis=1, keepdims=True)
    gene_id = iota((total, 1), 0)

    def chosen(where, value):
        return jnp.sum(jnp.where(where, value, 0), axis=0, keepdims=True)

    variant = iota((1, TV), 1)
    live = [
        jnp.where(variant < chosen((home_col == me) & (rank == s), len_col), 1.0, 0.0)
        for s in range(SLOTS)
    ]
    mask = jnp.concatenate(live, axis=1)
    far = home_col - me
    far = jnp.where(far < 0, far + ng, far)
    here = [chosen(gene_id == me * owned + o, far) for o in range(owned)]
    slot = [chosen(gene_id == me * owned + o, rank) for o in range(owned)]
    r, c = iota((16, SLOTS * ng * 8), 0), iota((16, SLOTS * ng * 8), 1)
    first = jnp.where(r < 8, r % 2, (r - 8) // 4) == 0
    at = jnp.where(first, here[0], here[1])
    s = jnp.where(first, slot[0], slot[1])
    line = jnp.where(r < 8, jnp.where(r < 2, 4, 5), r % 4)
    hit = (c == (s * ng + at) * 8 + line) & ((r < 4) | (r >= 8))
    return mask, jnp.where(hit, 1.0, 0.0)


def per_device(genotypes, covariates, proteins, gene_device, tile_len):
    ni, ng = lax.axis_size("ind"), lax.axis_size("gene")
    rows, pt = proteins.shape
    lanes = SLOTS * TV
    half = pt * ng // ni
    owned = gene_device.shape[0] // ng
    units = TILES if ni >= TILES else 6
    tall_unit = TILES // units * 8
    ny, nz = ni // NX, ng // 2
    vmem = pl.BlockSpec(memory_space=pltpu.VMEM)
    dma = pltpu.SemaphoreType.DMA
    unit = (SLOTS, ny * ROWS, TV)
    block = (SLOTS, ny, ROWS, TV)
    padded = ni // ng * ROWS
    scratch = [
        pltpu.VMEM((ny, NX, ROWS, TV), BF),
        pltpu.VMEM((ny // 2, NX, ROWS, TV), BF),
        pltpu.VMEM((ny // 2, NX, ROWS, TV), BF),
        pltpu.VMEM((ny // 2, NX, ROWS, TV), BF),
        pltpu.VMEM((ny // 2, NX, ROWS, TV), BF),
        pltpu.VMEM((NX, ROWS, TV), BF),
        pltpu.VMEM((NX, ROWS, TV), BF),
        pltpu.VMEM((rows, lanes), jnp.int32),
        pltpu.VMEM((rows, lanes), BF),
        pltpu.VMEM((rows, lanes), BF),
        pltpu.VMEM((32, rows), F32),
        pltpu.VMEM((96, rows), BF),
        pltpu.VMEM((rows, 256), BF),
        pltpu.VMEM((2, ng * padded, rows // 2), BF),
        pltpu.VMEM((units, tall_unit, TV), F32),
        pltpu.VMEM((ni, tall_unit, TV), F32),
        pltpu.VMEM((tall_unit, TV), F32),
        pltpu.VMEM((units, tall_unit, TV), F32),
        pltpu.VMEM((ng, 32, TV), BF),
        pltpu.VMEM((SLOTS, ni, 8, TV), F32),
        pltpu.VMEM((ni, 8, TV), F32),
        pltpu.VMEM((ny * ROWS, PAIR * TV), F32),
        pltpu.VMEM((SLOTS, NX, ny * ROWS, TV), BF),
        pltpu.VMEM(unit, BF),
        pltpu.VMEM(unit, BF),
        pltpu.VMEM(unit, BF),
        pltpu.VMEM(unit, BF),
        pltpu.VMEM(block, BF),
        pltpu.VMEM(block, BF),
        pltpu.VMEM((SLOTS, 8, TV), F32),
        pltpu.VMEM((SLOTS, ng, 8, TV), F32),
        dma((ny // 2,)), dma((ny // 2,)), dma((ny // 2,)), dma((ny // 2,)), dma, dma,
        dma,
        dma((2, nz // 2, 2)), dma((2, nz // 2, 2)),
        dma((2, nz // 2, 2)), dma((2, nz // 2, 2)),
        dma((2,)), dma((2,)), dma, dma, dma, dma, dma, dma,
        dma((SLOTS, 3)), dma((SLOTS, 3)),
        dma((SLOTS,)), dma((SLOTS,)),
        dma, dma, dma((SLOTS,)), dma((SLOTS,)),
    ]
    return pl.pallas_call(
        functools.partial(kernel, ni, ng, half, units),
        out_shape=(
            jax.ShapeDtypeStruct((owned, half), F32),
            jax.ShapeDtypeStruct((owned, half), F32),
            jax.ShapeDtypeStruct((owned, COV_ROWS, TV), F32),
        ),
        in_specs=[pl.BlockSpec(memory_space=pl.ANY), vmem, vmem, vmem, vmem],
        out_specs=(vmem, vmem, vmem),
        scratch_shapes=scratch,
        compiler_params=pltpu.CompilerParams(
            collective_id=0, has_side_effects=True, vmem_limit_bytes=66_000_000
        ),
    )(genotypes, covariates, proteins.T, gene_device[None, :], tile_len[None, :])


def solution(mesh):
    return jax.shard_map(
        per_device,
        mesh=mesh,
        in_specs=(P("ind", "gene"), P(None, "ind"), P("ind", "gene"), P(), P()),
        out_specs=(P("gene", "ind"), P("gene", "ind"), P("gene", "ind", None)),
        check_vma=False,
    )
```
